512 devices in a mesh: rows: 32 (over x, z), cols: 16 (over y, core).
Axes of the slice: x: 4, y: 8, z: 8, core: 2. Of those that a mesh axis runs over, the one named last changes fastest.
Arguments:
- features: bfloat16 [768, 512, 2048], P(None, 'rows', 'cols'), may hold values from -6 to 6
- labels: int32 [512, 2048], P('rows', 'cols'), may hold values from 0 to 15
- w_input: bfloat16 [128, 768], replicated, may hold values from -0.21875 to 0.21875
- w_dilate4: bfloat16 [128, 1152], replicated, may hold values from -0.1875 to 0.1875
- w_dilate8: bfloat16 [128, 1152], replicated, may hold values from -0.1875 to 0.1875
- w_classes: bfloat16 [16, 128], replicated, may hold values from -0.5 to 0.5
Outputs:
- grad_input: float32 [128, 768], replicated
- grad_dilate4: float32 [128, 1152], replicated
- grad_dilate8: float32 [128, 1152], replicated
- grad_classes: float32 [16, 128], replicated
The draws below stay inside these ranges and needn't reach their ends.
All inputs are finite; a program needn't handle non-finite values.
Results may differ from the reference program's by a relative error of at most 0.006.
Values may be sent and summed in bfloat16 or wider, within the bound.
No kernel may reach another device: no remote copies, remote signals or barrier semaphores. Data moves between devices by JAX's collectives and lax.ppermute only.
A program may use at most 128 MiB of HBM per device.

```python
import jax
import jax.numpy as jnp
from jax import lax

CH = 768
MID = 128
CLASSES = 16
HEIGHT = 512
WIDTH = 2048


def plant(result, rng, least, largest):
    place = [jax.random.randint(jax.random.fold_in(rng, axis), (), 0, length) for axis, length in enumerate(result.shape)]
    main_axis = result.shape.index(max(result.shape))
    beside = place[:main_axis] + [(place[main_axis] + 1) % result.shape[main_axis]] + place[main_axis + 1:]
    return result.at[tuple(place)].set(least).at[tuple(beside)].set(largest)


def level_of(stream_key, dims, cuts, least, largest):
    loudness = 1.0
    for position, shards_of in cuts:
        draws = jax.random.uniform(jax.random.fold_in(jax.random.fold_in(stream_key, 6), position), (shards_of,), jnp.float32, least / len(cuts), largest / len(cuts))
        loudness = loudness * jnp.repeat(jnp.exp(draws), dims[position] // shards_of).reshape((-1,) + (1,) * (len(dims) - 1 - position))
    return loudness


def bell_draw(rng, dims, scale, reach, cuts=(), kind=jnp.bfloat16):
    values = jax.random.normal(rng, dims, jnp.float32) * scale
    if len(cuts) > 0:
        values = level_of(rng, dims, cuts, -0.22, 0.18) * values
    return jnp.clip(values, min=-reach, max=reach).astype(kind)


def setup_inputs(seed: int = 0) -> dict:
    key_list = jax.random.split(jax.random.key(seed), 7)
    features = bell_draw(key_list[0], (CH, HEIGHT, WIDTH), 1.0, 6.0, ((1, 32), (2, 16)))
    labels = plant(jax.random.randint(key_list[1], (HEIGHT, WIDTH), 0, CLASSES), jax.random.fold_in(key_list[1], 1), 0, CLASSES - 1).astype(jnp.int32)
    w_input = bell_draw(key_list[2], (MID, CH), CH ** -0.5, 0.21875)
    w_dilate4 = bell_draw(key_list[3], (MID, 9 * MID), (9 * MID) ** -0.5, 0.1875)
    w_dilate8 = bell_draw(key_list[4], (MID, 9 * MID), (9 * MID) ** -0.5, 0.1875)
    w_classes = bell_draw(key_list[5], (CLASSES, MID), MID ** -0.5, 0.5)
    return {"features": features, "labels": labels, "w_input": w_input, "w_dilate4": w_dilate4, "w_dilate8": w_dilate8, "w_classes": w_classes}


loss_weight = 0.03125

def smooth(value):
    return value * jax.nn.sigmoid(value)

def slope(value):
    sig = jax.nn.sigmoid(value)
    return sig * (1.0 + value * (1.0 - sig))

def shifted(field, down, right):
    height = field.shape[1]
    width = field.shape[2]
    padded = jnp.pad(field, ((0, 0), (8, 8), (8, 8)))
    return padded[:, 8 + down:8 + down + height, 8 + right:8 + right + width]

def convolve(field, weight, dilation, sign):
    chans = field.shape[0]
    total = jnp.zeros((weight.shape[0], field.shape[1] * field.shape[2]), jnp.float32)
    for tap in range(9):
        piece = shifted(field, sign * (tap // 3 - 1) * dilation, sign * (tap % 3 - 1) * dilation)
        total = total + jnp.dot(weight[:, tap * chans:(tap + 1) * chans], piece.reshape(chans, -1), preferred_element_type=jnp.float32)
    return total

def pixel_contract(left, right):
    return lax.dot_general(left, right, (((1,), (1,)), ((), ())), preferred_element_type=jnp.float32)

def kernel_grad(grad, field, dilation):
    chans = field.shape[0]
    blocks = []
    for tap in range(9):
        piece = shifted(field, (tap // 3 - 1) * dilation, (tap % 3 - 1) * dilation)
        blocks.append(pixel_contract(grad, piece.reshape(chans, -1)))
    return jnp.concatenate(blocks, 1)

def flipped(weight):
    chans = weight.shape[0]
    return weight.reshape(chans, 9, chans).transpose(2, 1, 0).reshape(chans, 9 * chans)

def reference(features, labels, w_input, w_dilate4, w_dilate8, w_classes):
    flat = features.reshape(CH, -1)
    a1 = jnp.dot(w_input, flat, preferred_element_type=jnp.float32)
    h1 = smooth(a1).astype(jnp.bfloat16).reshape(MID, HEIGHT, WIDTH)
    a2 = convolve(h1, w_dilate4, 4, 1)
    h2 = smooth(a2).astype(jnp.bfloat16).reshape(MID, HEIGHT, WIDTH)
    a3 = convolve(h2, w_dilate8, 8, 1)
    h3 = smooth(a3).astype(jnp.bfloat16)
    logits = jnp.dot(w_classes, h3, preferred_element_type=jnp.float32)
    expo = jnp.exp(logits)
    prob = expo / lax.optimization_barrier(jnp.sum(expo, axis=0, keepdims=True))
    onehot = (labels.reshape(1, -1) == jnp.arange(CLASSES, dtype=jnp.int32)[:, None]).astype(jnp.float32)
    g4 = (loss_weight * (prob - onehot)).astype(jnp.bfloat16)
    grad_classes = pixel_contract(g4, h3)
    back3 = lax.dot_general(w_classes, g4, (((0,), (0,)), ((), ())), preferred_element_type=jnp.float32)
    g3 = (back3 * slope(a3)).astype(jnp.bfloat16)
    grad_dilate8 = kernel_grad(g3, h2, 8)
    back2 = convolve(g3.reshape(MID, HEIGHT, WIDTH), flipped(w_dilate8), 8, -1)
    g2 = (back2 * slope(a2)).astype(jnp.bfloat16)
    grad_dilate4 = kernel_grad(g2, h1, 4)
    back1 = convolve(g2.reshape(MID, HEIGHT, WIDTH), flipped(w_dilate4), 4, -1)
    g1 = (back1 * slope(a1)).astype(jnp.bfloat16)
    grad_input = pixel_contract(g1, flat)
    return (grad_input, grad_dilate4, grad_dilate8, grad_classes)
```

```python
import math

import jax
import jax.numpy as jnp
from jax import lax
from jax.experimental import pallas as pl
from jax.experimental.pallas import tpu as pltpu
from jax.sharding import Mesh, PartitionSpec as P

loss_weight = 0.03125
B = 4
H = 3
MID = 128
F32 = jnp.float32
BF16 = jnp.bfloat16


def vmem(n):
    return [pl.BlockSpec(memory_space=pltpu.VMEM)] * n


def call(body, name, outs, n_in, scratch=(), flops=0, smem=0, limit=56 << 20):
    shapes = [jax.ShapeDtypeStruct(s, d) for s, d in outs]
    size = sum(math.prod(s) * jnp.dtype(d).itemsize for s, d in outs)
    return pl.pallas_call(
        body,
        name=name,
        out_shape=shapes,
        in_specs=[pl.BlockSpec(memory_space=pltpu.SMEM)] * smem + vmem(n_in - smem),
        out_specs=vmem(len(outs)),
        scratch_shapes=list(scratch),
        compiler_params=pltpu.CompilerParams(vmem_limit_bytes=limit),
        cost_estimate=pl.CostEstimate(flops=flops, bytes_accessed=2 * size, transcendentals=0),
    )


def to_blocks(rows):
    cols, ch = rows[0].shape
    sub = lax.broadcasted_iota(jnp.int32, (cols // 8, 8, ch), 1)

    def pair(low, high):
        low, high = low.reshape(cols // 8, 8, ch), high.reshape(cols // 8, 8, ch)
        even = jnp.where(sub < 4, low, pltpu.roll(high, 4, 1))
        odd = jnp.where(sub < 4, pltpu.roll(low, 4, 1), high)
        return jnp.stack([even, odd], 1).reshape(cols // 4, 8, ch)

    return jnp.concatenate([pair(rows[0], rows[1]), pair(rows[2], rows[3])], 1)


def from_blocks(tile):
    blocks, _, ch = tile.shape
    sub = lax.broadcasted_iota(jnp.int32, (blocks // 2, 8, ch), 1)
    rows = []
    for half in range(2):
        v = tile[:, half * 8 : half * 8 + 8, :].reshape(blocks // 2, 2, 8, ch)
        even, odd = v[:, 0], v[:, 1]
        low = jnp.where(sub < 4, even, pltpu.roll(odd, 4, 1))
        high = jnp.where(sub < 4, pltpu.roll(even, 4, 1), odd)
        rows += [low.reshape(blocks * 4, ch), high.reshape(blocks * 4, ch)]
    return rows


def sigmoid(a):
    return 1.0 / (1.0 + jnp.exp(-a))


def dot(a, b, ca, cb):
    return lax.dot_general(a, b, (((ca,), (cb,)), ((), ())), preferred_element_type=F32)


def squeeze_kernel(a1_ref, h1_ref, top_ref, bottom_ref):
    rb, cb = h1_ref.shape[0], h1_ref.shape[1]
    cols = cb * B
    for i in range(rb):
        rows = [a1_ref[:, (i * B + r) * cols : (i * B + r + 1) * cols].T for r in range(B)]
        a = to_blocks(rows)
        h = (a * sigmoid(a)).astype(BF16)
        h1_ref[i] = h
        if i < H:
            top_ref[i] = h
        if i >= rb - H:
            bottom_ref[i - (rb - H)] = h


def taps(ref, row, step, col, n, sign=1):
    pieces = []
    for ky in range(3):
        for kx in range(3):
            dy, dx = (ky, kx) if sign > 0 else (2 - ky, 2 - kx)
            piece = ref[row + dy * step, col + dx * step : col + dx * step + n]
            pieces.append(piece.reshape(n * 16, piece.shape[-1]))
    return jnp.concatenate(pieces, 1)


def transposed(w_ref, out_ref):
    for t in range(9):
        w = w_ref[:, t * MID : (t + 1) * MID].astype(F32)
        out_ref[t * MID : (t + 1) * MID, :] = w.T.astype(BF16)


def stacked(w_ref, out_ref):
    for t in range(9):
        out_ref[t * MID : (t + 1) * MID, :] = w_ref[:, t * MID : (t + 1) * MID]


def inside(pos_ref, row, col, n, rb, cb):
    rows = pos_ref[0] * rb + row
    cols = pos_ref[1] * cb + col + lax.broadcasted_iota(jnp.int32, (n * 16, 1), 0) // 16
    rows = jnp.broadcast_to(rows, cols.shape)
    return (rows >= 0) & (rows < pos_ref[2]) & (cols >= 0) & (cols < pos_ref[3])


def fill(pad_ref, own_ref, up_ref, down_ref, left_ref, right_ref):
    rb, cb = own_ref.shape[0], own_ref.shape[1]
    pad_ref[:H, H : H + cb] = up_ref[...]
    pad_ref[H : H + rb, H : H + cb] = own_ref[...]
    pad_ref[H + rb :, H : H + cb] = down_ref[...]
    pad_ref[:, :H] = left_ref[...]
    pad_ref[:, H + cb :] = right_ref[...]


def forward_kernel(pos_ref, own_ref, up_ref, down_ref, left_ref, right_ref, w4_ref, w8_ref, wc_ref, labels_ref,
                   g3_ref, top_ref, bottom_ref, h1_ref, h2_ref, slope2_ref, gc_ref, w4t_ref, w8t_ref):
    rb, cb = own_ref.shape[0], own_ref.shape[1]
    fill(h1_ref, own_ref, up_ref, down_ref, left_ref, right_ref)
    transposed(w4_ref, w4t_ref)
    transposed(w8_ref, w8t_ref)
    n = cb + 4

    def first(i, carry):
        a = jnp.dot(taps(h1_ref, i, 1, 0, n), w4t_ref[...], preferred_element_type=F32)
        s = sigmoid(a)
        h = jnp.where(inside(pos_ref, i - 2, -2, n, rb, cb), a * s, 0.0)
        h2_ref[i] = h.astype(BF16).reshape(n, 16, MID)
        slope2_ref[i] = (s * (1.0 + a * (1.0 - s))).reshape(n, 16, MID)
        return carry

    lax.fori_loop(0, rb + 4, first, 0)
    gc_ref[...] = jnp.zeros_like(gc_ref)
    px = cb * 16
    wc = wc_ref[...]
    classes = wc.shape[0]
    for i in range(rb):
        a = jnp.dot(taps(h2_ref, i, 2, 0, cb), w8t_ref[...], preferred_element_type=F32)
        s = sigmoid(a)
        h3 = (a * s).astype(BF16)
        expo = jnp.exp(dot(wc, h3, 1, 1))
        prob = expo / jnp.sum(expo, axis=0, keepdims=True)
        label = labels_ref[:, i * px : (i + 1) * px]
        hot = (label == lax.broadcasted_iota(jnp.int32, (classes, px), 0)).astype(F32)
        g4 = (loss_weight * (prob - hot)).astype(BF16)
        gc_ref[...] += jnp.dot(g4, h3, preferred_element_type=F32)
        back = dot(g4, wc, 0, 0)
        g3 = (back * (s * (1.0 + a * (1.0 - s)))).astype(BF16).reshape(cb, 16, MID)
        g3_ref[i] = g3
        if i < H:
            top_ref[i] = g3
        if i >= rb - H:
            bottom_ref[i - (rb - H)] = g3


def dilate8_kernel(g3_ref, h2_ref, out_ref, acc_ref):
    rb, cb = g3_ref.shape[0], g3_ref.shape[1]
    for i in range(rb):
        g = g3_ref[i].reshape(cb * 16, MID)
        part = dot(g, taps(h2_ref, i, 2, 0, cb), 0, 0)
        if i == 0:
            acc_ref[...] = part
        else:
            acc_ref[...] += part
    for t in range(9):
        out_ref[t * MID : (t + 1) * MID, :] = acc_ref[:, t * MID : (t + 1) * MID].astype(BF16)


def backward_kernel(pos_ref, own_ref, up_ref, down_ref, left_ref, right_ref, w4_ref, w8_ref, h1_ref, slope2_ref,
                    a1_ref, g1_ref, out_ref, g3_ref, g2_ref, w4s_ref, w8s_ref, acc_ref):
    rb, cb = own_ref.shape[0], own_ref.shape[1]
    cols = cb * B
    fill(g3_ref, own_ref, up_ref, down_ref, left_ref, right_ref)
    stacked(w4_ref, w4s_ref)
    stacked(w8_ref, w8s_ref)
    n = cb + 2

    def first(i, carry):
        back = jnp.dot(taps(g3_ref, i, 2, 0, n, -1), w8s_ref[...], preferred_element_type=F32)
        g = back * slope2_ref[i + 1, 1 : 1 + n].reshape(n * 16, MID)
        g = jnp.where(inside(pos_ref, i - 1, -1, n, rb, cb), g, 0.0)
        g2_ref[i] = g.astype(BF16).reshape(n, 16, MID)
        return carry

    lax.fori_loop(0, rb + 2, first, 0)
    for i in range(rb):
        g = g2_ref[i + 1, 1 : 1 + cb].reshape(cb * 16, MID)
        part = dot(g, taps(h1_ref, i + 2, 1, 2, cb), 0, 0)
        if i == 0:
            acc_ref[...] = part
        else:
            acc_ref[...] += part
        back = jnp.dot(taps(g2_ref, i, 1, 0, cb, -1), w4s_ref[...], preferred_element_type=F32)
        for r, row in enumerate(from_blocks(back.reshape(cb, 16, MID))):
            at = (i * B + r) * cols
            a = a1_ref[:, at : at + cols]
            s = sigmoid(a)
            g1_ref[:, at : at + cols] = (row.T * (s * (1.0 + a * (1.0 - s)))).astype(BF16)
    for t in range(9):
        out_ref[t * MID : (t + 1) * MID, :] = acc_ref[:, t * MID : (t + 1) * MID].astype(BF16)


def pack_kernel(gi_ref, g4_ref, g8_ref, gc_ref, out_ref):
    at = 0
    for t in range(gi_ref.shape[1] // MID):
        out_ref[at : at + MID, :] = gi_ref[:, t * MID : (t + 1) * MID].astype(BF16)
        at += MID
    for ref in (g4_ref, g8_ref, gc_ref):
        out_ref[at : at + ref.shape[0], :] = ref[...].astype(BF16)
        at += ref.shape[0]
    out_ref[at:, :] = jnp.zeros((out_ref.shape[0] - at, MID), BF16)


def unpack_kernel(cores, part_ref, gi_ref, g4_ref, g8_ref, gc_ref):
    groups, length, _ = part_ref.shape
    outer = groups // cores

    def piece(start, count):
        got = []
        while count:
            chunk, offset = divmod(start, length)
            size = min(count, length - offset)
            core, y = divmod(chunk, outer)
            got.append(part_ref[y * cores + core, offset : offset + size, :].astype(F32))
            start, count = start + size, count - size
        return got[0] if len(got) == 1 else jnp.concatenate(got, 0)

    at = 0
    for ref in (gi_ref, g4_ref, g8_ref):
        for t in range(ref.shape[1] // MID):
            ref[:, t * MID : (t + 1) * MID] = piece(at, MID)
            at += MID
    gc_ref[...] = piece(at, gc_ref.shape[0])


ROWS, COLS = ("x", "z"), ("y", "c")


def neighbour(value, axes, step):
    count = lax.axis_size(axes)
    pairs = [(i, i + step) for i in range(count) if 0 <= i + step < count]
    return lax.ppermute(value, axes, pairs)


def halos(own, top, bottom):
    up = neighbour(bottom, ROWS, 1)
    down = neighbour(top, ROWS, -1)
    cb = own.shape[1]

    def side(first):
        return jnp.concatenate([lax.slice_in_dim(v, first, first + H, axis=1) for v in (up, own, down)], 0)

    left = neighbour(side(cb - H), COLS, 1)
    right = neighbour(side(0), COLS, -1)
    return up, down, left, right


def over_devices(packed, unit):
    cores, ys, xz = lax.axis_size("c"), lax.axis_size("y"), lax.axis_size(ROWS)

    def exchange(v, axes, n):
        v = lax.all_to_all(v.reshape(n, -1, MID), axes, 0, 0, tiled=True)
        return jnp.sum(v.astype(F32), 0).astype(BF16)

    part = exchange(packed, "c", cores)
    part = exchange(part, ("y",) + ROWS, ys * xz)
    part = jnp.broadcast_to(part[None], (xz,) + part.shape)
    part = lax.all_to_all(part, ROWS, 0, 0, tiled=True)
    part = lax.all_gather(part.reshape(1, xz * unit, MID), COLS, axis=0, tiled=True)
    return part


def local(features, labels, w_input, w_dilate4, w_dilate8, w_classes):
    chans, rows, cols = features.shape
    rb, cb = rows // B, cols // B
    px = rows * cols
    classes = w_classes.shape[0]
    devices = lax.axis_size(ROWS + COLS)
    conv = 2 * 9 * MID * MID * px

    pos = jnp.stack([
        lax.axis_index(ROWS), lax.axis_index(COLS),
        jnp.int32(rb * lax.axis_size(ROWS)), jnp.int32(cb * lax.axis_size(COLS)),
    ]).astype(jnp.int32)
    order = labels.reshape(rb, B, cb, B).transpose(0, 2, 1, 3).reshape(1, px)

    a1 = jnp.dot(w_input, features.reshape(chans, px), preferred_element_type=F32)
    edge = ((H, cb, 16, MID), BF16)
    tile = ((rb, cb, 16, MID), BF16)
    h1, top, bottom = call(squeeze_kernel, "squeeze", [tile, edge, edge], 1, flops=px * MID)(a1)
    up, down, left, right = halos(h1, top, bottom)

    padded = ((rb + 2 * H, cb + 2 * H, 16, MID), BF16)
    weight = pltpu.VMEM((9 * MID, MID), BF16)
    g3, top, bottom, h1_pad, h2_pad, slope2, gc = call(
        forward_kernel, "forward",
        [tile, edge, edge, padded, ((rb + 4, cb + 4, 16, MID), BF16), ((rb + 4, cb + 4, 16, MID), F32),
         ((classes, MID), F32)],
        10, [weight, weight], flops=4 * conv, smem=1,
    )(pos, h1, up, down, left, right, w_dilate4, w_dilate8, w_classes, order)
    up, down, left, right = halos(g3, top, bottom)
    acc = pltpu.VMEM((MID, 9 * MID), F32)
    (g8,) = call(dilate8_kernel, "dilate8", [((9 * MID, MID), BF16)], 2, [acc], flops=conv)(g3, h2_pad)
    g1, g4 = call(
        backward_kernel, "backward",
        [((MID, px), BF16), ((9 * MID, MID), BF16)],
        11, [pltpu.VMEM(*padded), pltpu.VMEM((rb + 2, cb + 2, 16, MID), BF16), weight, weight, acc],
        flops=4 * conv, smem=1,
    )(pos, g3, up, down, left, right, w_dilate4, w_dilate8, h1_pad, slope2, a1)
    gi = lax.dot_general(
        g1.reshape(MID, rows, cols), features, (((1, 2), (1, 2)), ((), ())), preferred_element_type=F32
    )

    used = MID * (chans // MID + 18) + classes
    unit = -(-used // (8 * devices)) * 8
    (packed,) = call(pack_kernel, "pack", [((unit * devices, MID), BF16)], 4)(gi, g4, g8, gc)
    part = over_devices(packed, unit)
    return tuple(call(
        lambda *refs: unpack_kernel(lax.axis_size("c"), *refs), "unpack",
        [((MID, chans), F32), ((MID, 9 * MID), F32), ((MID, 9 * MID), F32), ((classes, MID), F32)], 1,
    )(part))


def solution(mesh):
    rows, cols = mesh.shape["rows"], mesh.shape["cols"]
    inner = math.gcd(rows, 8)
    torus = Mesh(mesh.devices.reshape(rows // inner, inner, cols // 2, 2), ROWS + COLS)
    return jax.shard_map(
        local,
        mesh=torus,
        in_specs=(P(None, ROWS, COLS), P(ROWS, COLS), P(), P(), P(), P()),
        out_specs=(P(), P(), P(), P()),
        check_vma=False,
    )
```

```python
import math

import jax
import jax.numpy as jnp
from jax import lax
from jax.experimental import pallas as pl
from jax.experimental.pallas import tpu as pltpu
from jax.sharding import Mesh, PartitionSpec as P

loss_weight = 0.03125
B = 4
H = 3
MID = 128
F32 = jnp.float32
BF16 = jnp.bfloat16


def vmem(n):
    return [pl.BlockSpec(memory_space=pltpu.VMEM)] * n


def call(body, name, outs, n_in, scratch=(), flops=0, smem=0, limit=20 << 20):
    shapes = [jax.ShapeDtypeStruct(s, d) for s, d in outs]
    size = sum(math.prod(s) * jnp.dtype(d).itemsize for s, d in outs)
    return pl.pallas_call(
        body,
        name=name,
        out_shape=shapes,
        in_specs=[pl.BlockSpec(memory_space=pltpu.SMEM)] * smem + vmem(n_in - smem),
        out_specs=vmem(len(outs)),
        scratch_shapes=list(scratch),
        compiler_params=pltpu.CompilerParams(vmem_limit_bytes=limit),
        cost_estimate=pl.CostEstimate(flops=flops, bytes_accessed=2 * size, transcendentals=0),
    )


def to_blocks(rows):
    cols, ch = rows[0].shape
    sub = lax.broadcasted_iota(jnp.int32, (cols // 8, 8, ch), 1)

    def pair(low, high):
        low, high = low.reshape(cols // 8, 8, ch), high.reshape(cols // 8, 8, ch)
        even = jnp.where(sub < 4, low, pltpu.roll(high, 4, 1))
        odd = jnp.where(sub < 4, pltpu.roll(low, 4, 1), high)
        return jnp.stack([even, odd], 1).reshape(cols // 4, 8, ch)

    return jnp.concatenate([pair(rows[0], rows[1]), pair(rows[2], rows[3])], 1)


def from_blocks(tile):
    blocks, _, ch = tile.shape
    sub = lax.broadcasted_iota(jnp.int32, (blocks // 2, 8, ch), 1)
    rows = []
    for half in range(2):
        v = tile[:, half * 8 : half * 8 + 8, :].reshape(blocks // 2, 2, 8, ch)
        even, odd = v[:, 0], v[:, 1]
        low = jnp.where(sub < 4, even, pltpu.roll(odd, 4, 1))
        high = jnp.where(sub < 4, pltpu.roll(even, 4, 1), odd)
        rows += [low.reshape(blocks * 4, ch), high.reshape(blocks * 4, ch)]
    return rows


def sigmoid(a):
    return 1.0 / (1.0 + jnp.exp(-a))


def dot(a, b, ca, cb):
    return lax.dot_general(a, b, (((ca,), (cb,)), ((), ())), preferred_element_type=F32)


def squeeze_kernel(a1_ref, h1_ref, top_ref, bottom_ref):
    rb, cb = h1_ref.shape[0], h1_ref.shape[1]
    cols = cb * B
    for i in range(rb):
        rows = [a1_ref[:, (i * B + r) * cols : (i * B + r + 1) * cols].T for r in range(B)]
        a = to_blocks(rows)
        h = (a * sigmoid(a)).astype(BF16)
        h1_ref[i] = h
        if i < H:
            top_ref[i] = h
        if i >= rb - H:
            bottom_ref[i - (rb - H)] = h


def taps(ref, row, step, col, n, slots=3):
    pieces = []
    for dy in range(slots):
        for dx in range(3):
            piece = ref[row + dy * step, col + dx * step : col + dx * step + n]
            pieces.append(piece.reshape(n * 16, piece.shape[-1]))
    return jnp.concatenate(pieces, 1)


def pair_weights(w_ref, out_ref, back):
    zero = jnp.zeros((MID, MID), BF16)
    for dy in range(4):
        for dx in range(3):
            for side in range(2):
                ky, kx = (2 - dy + side, 2 - dx) if back else (dy - side, dx)
                tap = zero
                if 0 <= ky < 3:
                    at = (3 * ky + kx) * MID
                    tap = w_ref[:, at : at + MID]
                    if not back:
                        tap = tap.astype(F32).T.astype(BF16)
                at = (3 * dy + dx) * MID
                out_ref[at : at + MID, side * MID : (side + 1) * MID] = tap


def inside(pos_ref, row, col, n, rb, cb):
    rows = pos_ref[0] * rb + row
    cols = pos_ref[1] * cb + col + lax.broadcasted_iota(jnp.int32, (n * 16, 1), 0) // 16
    rows = jnp.broadcast_to(rows, cols.shape)
    return (rows >= 0) & (rows < pos_ref[2]) & (cols >= 0) & (cols < pos_ref[3])


def fill(pad_ref, own_ref, up_ref, down_ref, left_ref, right_ref):
    rb, cb = own_ref.shape[0], own_ref.shape[1]
    pad_ref[:H, H : H + cb] = up_ref[...]
    pad_ref[H : H + rb, H : H + cb] = own_ref[...]
    pad_ref[H + rb :, H : H + cb] = down_ref[...]
    pad_ref[:, :H] = left_ref[...]
    pad_ref[:, H + cb :] = right_ref[...]


def forward_kernel(pos_ref, own_ref, up_ref, down_ref, left_ref, right_ref, w4_ref, w8_ref, wc_ref, labels_ref,
                   g3_ref, top_ref, bottom_ref, h1_ref, h2_ref, slope2_ref, gc_ref, w4t_ref, w8t_ref):
    rb, cb = own_ref.shape[0], own_ref.shape[1]
    fill(h1_ref, own_ref, up_ref, down_ref, left_ref, right_ref)
    pair_weights(w4_ref, w4t_ref, False)
    pair_weights(w8_ref, w8t_ref, False)
    n = cb + 4

    def first(j, carry):
        both = jnp.dot(taps(h1_ref, 2 * j, 1, 0, n, 4), w4t_ref[...], preferred_element_type=F32)
        for side in range(2):
            i = 2 * j + side
            a = both[:, side * MID : (side + 1) * MID]
            s = sigmoid(a)
            h = jnp.where(inside(pos_ref, i - 2, -2, n, rb, cb), a * s, 0.0)
            h2_ref[i] = h.astype(BF16).reshape(n, 16, MID)
            slope2_ref[i] = (s * (1.0 + a * (1.0 - s))).reshape(n, 16, MID)
        return carry

    lax.fori_loop(0, (rb + 4) // 2, first, 0)
    gc_ref[...] = jnp.zeros_like(gc_ref)
    px = cb * 16
    wc = wc_ref[...]
    classes = wc.shape[0]
    for start in range(0, rb, 4):
        for j in (start, start + 1):
            both = jnp.dot(taps(h2_ref, j, 2, 0, cb, 4), w8t_ref[...], preferred_element_type=F32)
            for side in range(2):
                i = j + 2 * side
                a = both[:, side * MID : (side + 1) * MID]
                s = sigmoid(a)
                h3 = (a * s).astype(BF16)
                expo = jnp.exp(dot(wc, h3, 1, 1))
                prob = expo / jnp.sum(expo, axis=0, keepdims=True)
                label = labels_ref[:, i * px : (i + 1) * px]
                hot = (label == lax.broadcasted_iota(jnp.int32, (classes, px), 0)).astype(F32)
                g4 = (loss_weight * (prob - hot)).astype(BF16)
                gc_ref[...] += jnp.dot(g4, h3, preferred_element_type=F32)
                back = dot(g4, wc, 0, 0)
                g3 = (back * (s * (1.0 + a * (1.0 - s)))).astype(BF16).reshape(cb, 16, MID)
                g3_ref[i] = g3
                if i < H:
                    top_ref[i] = g3
                if i >= rb - H:
                    bottom_ref[i - (rb - H)] = g3


def dilate8_kernel(g3_ref, h2_ref, out_ref, acc_ref):
    rb, cb = g3_ref.shape[0], g3_ref.shape[1]
    for i in range(rb):
        g = g3_ref[i].reshape(cb * 16, MID)
        part = dot(g, taps(h2_ref, i, 2, 0, cb), 0, 0)
        if i == 0:
            acc_ref[...] = part
        else:
            acc_ref[...] += part
    for t in range(9):
        out_ref[t * MID : (t + 1) * MID, :] = acc_ref[:, t * MID : (t + 1) * MID].astype(BF16)


def backward_kernel(pos_ref, own_ref, up_ref, down_ref, left_ref, right_ref, w4_ref, w8_ref, h1_ref, slope2_ref,
                    a1_ref, g1_ref, out_ref, g3_ref, g2_ref, w4s_ref, w8s_ref, acc_ref):
    rb, cb = own_ref.shape[0], own_ref.shape[1]
    cols = cb * B
    fill(g3_ref, own_ref, up_ref, down_ref, left_ref, right_ref)
    pair_weights(w4_ref, w4s_ref, True)
    pair_weights(w8_ref, w8s_ref, True)
    n = cb + 2

    def second(back, i):
        g = back * slope2_ref[i + 1, 1 : 1 + n].reshape(n * 16, MID)
        g = jnp.where(inside(pos_ref, i - 1, -1, n, rb, cb), g, 0.0)
        g2_ref[i] = g.astype(BF16).reshape(n, 16, MID)

    for i in range(0, rb + 2, 4):
        for j in range(i, min(i + 2, rb + 2)):
            if j + 2 < rb + 2:
                both = jnp.dot(taps(g3_ref, j, 2, 0, n, 4), w8s_ref[...], preferred_element_type=F32)
                second(both[:, :MID], j)
                second(both[:, MID:], j + 2)
            else:
                one = w8s_ref[: 9 * MID, :MID]
                second(jnp.dot(taps(g3_ref, j, 2, 0, n), one, preferred_element_type=F32), j)
    for j in range(0, rb, 2):
        both = jnp.dot(taps(g2_ref, j, 1, 0, cb, 4), w4s_ref[...], preferred_element_type=F32)
        for side in range(2):
            i = j + side
            g = g2_ref[i + 1, 1 : 1 + cb].reshape(cb * 16, MID)
            part = dot(g, taps(h1_ref, i + 2, 1, 2, cb), 0, 0)
            if i == 0:
                acc_ref[...] = part
            else:
                acc_ref[...] += part
            back = both[:, side * MID : (side + 1) * MID]
            for r, row in enumerate(from_blocks(back.reshape(cb, 16, MID))):
                at = (i * B + r) * cols
                a = a1_ref[:, at : at + cols]
                s = sigmoid(a)
                g1_ref[:, at : at + cols] = (row.T * (s * (1.0 + a * (1.0 - s)))).astype(BF16)
    for t in range(9):
        out_ref[t * MID : (t + 1) * MID, :] = acc_ref[:, t * MID : (t + 1) * MID].astype(BF16)


def spans(start, count, length):
    while count:
        group, offset = divmod(start, length)
        size = min(count, length - offset)
        yield group, offset, size
        start, count = start + size, count - size


def pack_kernel(length, gi_ref, g4_ref, g8_ref, gc_ref, out_ref):
    groups = out_ref.shape[0]

    def put(at, value):
        done = 0
        for group, offset, size in spans(at, value.shape[0], length):
            out_ref[group, offset : offset + size, :] = value[done : done + size]
            done += size
        return at + done

    at = 0
    for t in range(gi_ref.shape[1] // MID):
        at = put(at, gi_ref[:, t * MID : (t + 1) * MID].astype(BF16))
    for ref in (g4_ref, g8_ref, gc_ref):
        at = put(at, ref[...].astype(BF16))
    put(at, jnp.zeros((groups * length - at, MID), BF16))
    for group in range(groups):
        out_ref[group, length:, :] = jnp.zeros((out_ref.shape[1] - length, MID), BF16)


def unpack_kernel(cores, part_ref, gi_ref, g4_ref, g8_ref, gc_ref):
    groups, length, _ = part_ref.shape
    outer = groups // cores

    def piece(at, count):
        got = [
            part_ref[group % outer * cores + group // outer, offset : offset + size, :].astype(F32)
            for group, offset, size in spans(at, count, length)
        ]
        return got[0] if len(got) == 1 else jnp.concatenate(got, 0)

    at = 0
    for ref in (gi_ref, g4_ref, g8_ref):
        for t in range(ref.shape[1] // MID):
            ref[:, t * MID : (t + 1) * MID] = piece(at, MID)
            at += MID
    gc_ref[...] = piece(at, gc_ref.shape[0])


ROWS, COLS = ("x", "z"), ("y", "c")
PLANE = ("z", "x")


def neighbour(value, axes, step):
    count = lax.axis_size(axes)
    pairs = [(i, i + step) for i in range(count) if 0 <= i + step < count]
    return lax.ppermute(value, axes, pairs)


def halos(own, top, bottom, beside=None):
    up = neighbour(bottom, ROWS, 1)
    down = neighbour(top, ROWS, -1)
    cb = own.shape[1]
    done = None
    if beside is not None:
        done = beside(own)
        own, done = lax.optimization_barrier((own, done))

    def side(first):
        return jnp.concatenate([lax.slice_in_dim(v, first, first + H, axis=1) for v in (up, own, down)], 0)

    left = neighbour(side(cb - H), COLS, 1)
    right = neighbour(side(0), COLS, -1)
    return (up, down, left, right), done


def over_devices(packed, length):
    cores, ys, plane = lax.axis_size("c"), lax.axis_size("y"), lax.axis_size(PLANE)

    def exchange(v, axes, n):
        v = lax.all_to_all(v.reshape(n, -1, MID), axes, 0, 0, tiled=True)
        return jnp.sum(v.astype(F32), 0).astype(BF16)

    part = exchange(packed, "c", cores)
    part = exchange(part, ("y",) + PLANE, ys * plane)
    part = jnp.broadcast_to(part[None], (plane,) + part.shape)
    part = lax.all_to_all(part, PLANE, 0, 0, tiled=True)
    part = lax.all_gather(part.reshape(-1, MID)[:length], COLS, axis=0, tiled=True)
    return part.reshape(ys * cores, length, MID)


def local(features, labels, w_input, w_dilate4, w_dilate8, w_classes):
    chans, rows, cols = features.shape
    rb, cb = rows // B, cols // B
    px = rows * cols
    classes = w_classes.shape[0]
    conv = 2 * 9 * MID * MID * px

    pos = jnp.stack([
        lax.axis_index(ROWS), lax.axis_index(COLS),
        jnp.int32(rb * lax.axis_size(ROWS)), jnp.int32(cb * lax.axis_size(COLS)),
    ]).astype(jnp.int32)
    order = labels.reshape(rb, B, cb, B).transpose(0, 2, 1, 3).reshape(1, px)

    a1 = jnp.dot(w_input, features.reshape(chans, px), preferred_element_type=F32)
    edge = ((H, cb, 16, MID), BF16)
    tile = ((rb, cb, 16, MID), BF16)
    h1, top, bottom = call(squeeze_kernel, "squeeze", [tile, edge, edge], 1, flops=px * MID)(a1)
    around, _ = halos(h1, top, bottom)

    padded = ((rb + 2 * H, cb + 2 * H, 16, MID), BF16)
    weight = pltpu.VMEM((12 * MID, 2 * MID), BF16)
    g3, top, bottom, h1_pad, h2_pad, slope2, gc = call(
        forward_kernel, "forward",
        [tile, edge, edge, padded, ((rb + 4, cb + 4, 16, MID), BF16), ((rb + 4, cb + 4, 16, MID), F32),
         ((classes, MID), F32)],
        10, [weight, weight], flops=4 * conv, smem=1,
    )(pos, h1, *around, w_dilate4, w_dilate8, w_classes, order)
    acc = pltpu.VMEM((MID, 9 * MID), F32)
    dilate8 = call(dilate8_kernel, "dilate8", [((9 * MID, MID), BF16)], 2, [acc], flops=conv)
    around, (g8,) = halos(g3, top, bottom, lambda own: dilate8(own, h2_pad))
    g1, g4 = call(
        backward_kernel, "backward",
        [((MID, px), BF16), ((9 * MID, MID), BF16)],
        11, [pltpu.VMEM(*padded), pltpu.VMEM((rb + 2, cb + 2, 16, MID), BF16), weight, weight, acc],
        flops=4 * conv, smem=1,
    )(pos, g3, *around, w_dilate4, w_dilate8, h1_pad, slope2, a1)
    gi = lax.dot_general(
        g1.reshape(MID, rows, cols), features, (((1, 2), (1, 2)), ((), ())), preferred_element_type=F32
    )

    used = MID * (chans // MID + 18) + classes
    groups = lax.axis_size(COLS)
    length = -(-used // (16 * groups)) * 16
    unit = -(-length // (8 * lax.axis_size(PLANE))) * 8
    (packed,) = call(
        lambda *refs: pack_kernel(length, *refs), "pack",
        [((groups, unit * lax.axis_size(PLANE), MID), BF16)], 4,
    )(gi, g4, g8, gc)
    part = over_devices(packed, length)
    return tuple(call(
        lambda *refs: unpack_kernel(lax.axis_size("c"), *refs), "unpack",
        [((MID, chans), F32), ((MID, 9 * MID), F32), ((MID, 9 * MID), F32), ((classes, MID), F32)], 1,
    )(part))


def solution(mesh):
    rows, cols = mesh.shape["rows"], mesh.shape["cols"]
    inner = math.gcd(rows, 8)
    torus = Mesh(mesh.devices.reshape(rows // inner, inner, cols // 2, 2), ROWS + COLS)
    return jax.shard_map(
        local,
        mesh=torus,
        in_specs=(P(None, ROWS, COLS), P(ROWS, COLS), P(), P(), P(), P()),
        out_specs=(P(), P(), P(), P()),
        check_vma=False,
    )
```

```python
import math

import jax
import jax.numpy as jnp
from jax import lax
from jax.experimental import pallas as pl
from jax.experimental.pallas import tpu as pltpu
from jax.sharding import Mesh, PartitionSpec as P

loss_weight = 0.03125
B = 4
H = 3
MID = 128
SIDES = ((1, 0), (-1, 0), (0, 1), (0, -1), (1, 1), (1, -1), (-1, 1), (-1, -1))
F32 = jnp.float32
BF16 = jnp.bfloat16


def vmem(n):
    return [pl.BlockSpec(memory_space=pltpu.VMEM)] * n


def call(body, name, outs, n_in, scratch=(), flops=0, smem=0, limit=20 << 20):
    shapes = [jax.ShapeDtypeStruct(s, d) for s, d in outs]
    size = sum(math.prod(s) * jnp.dtype(d).itemsize for s, d in outs)
    return pl.pallas_call(
        body,
        name=name,
        out_shape=shapes,
        in_specs=[pl.BlockSpec(memory_space=pltpu.SMEM)] * smem + vmem(n_in - smem),
        out_specs=vmem(len(outs)),
        scratch_shapes=list(scratch),
        compiler_params=pltpu.CompilerParams(vmem_limit_bytes=limit),
        cost_estimate=pl.CostEstimate(flops=flops, bytes_accessed=2 * size, transcendentals=0),
    )


def to_blocks(rows):
    cols, ch = rows[0].shape
    sub = lax.broadcasted_iota(jnp.int32, (cols // 8, 8, ch), 1)

    def pair(low, high):
        low, high = low.reshape(cols // 8, 8, ch), high.reshape(cols // 8, 8, ch)
        even = jnp.where(sub < 4, low, pltpu.roll(high, 4, 1))
        odd = jnp.where(sub < 4, pltpu.roll(low, 4, 1), high)
        return jnp.stack([even, odd], 1).reshape(cols // 4, 8, ch)

    return jnp.concatenate([pair(rows[0], rows[1]), pair(rows[2], rows[3])], 1)


def from_blocks(tile):
    blocks, _, ch = tile.shape
    sub = lax.broadcasted_iota(jnp.int32, (blocks // 2, 8, ch), 1)
    rows = []
    for half in range(2):
        v = tile[:, half * 8 : half * 8 + 8, :].reshape(blocks // 2, 2, 8, ch)
        even, odd = v[:, 0], v[:, 1]
        low = jnp.where(sub < 4, even, pltpu.roll(odd, 4, 1))
        high = jnp.where(sub < 4, pltpu.roll(even, 4, 1), odd)
        rows += [low.reshape(blocks * 4, ch), high.reshape(blocks * 4, ch)]
    return rows


def sigmoid(a):
    return 1.0 / (1.0 + jnp.exp(-a))


def dot(a, b, ca, cb):
    return lax.dot_general(a, b, (((ca,), (cb,)), ((), ())), preferred_element_type=F32)


def edge_shapes(rb, cb):
    return [((H if dr else rb, H if dc else cb, 16, MID), BF16) for dr, dc in SIDES]


def put_edges(refs, i, row, rb):
    cb = row.shape[0]
    for ref, (dr, dc) in zip(refs, SIDES):
        piece = row[:H] if dc < 0 else row[cb - H :] if dc > 0 else row
        if dr == 0:
            ref[i] = piece
        elif dr < 0 and i < H:
            ref[i] = piece
        elif dr > 0 and i >= rb - H:
            ref[i - (rb - H)] = piece


def squeeze_kernel(a1_ref, h1_ref, *edge_refs):
    rb, cb = h1_ref.shape[0], h1_ref.shape[1]
    cols = cb * B
    for i in range(rb):
        rows = [a1_ref[:, (i * B + r) * cols : (i * B + r + 1) * cols].T for r in range(B)]
        a = to_blocks(rows)
        h = (a * sigmoid(a)).astype(BF16)
        h1_ref[i] = h
        put_edges(edge_refs, i, h, rb)


def taps(ref, row, step, col, n, slots=3):
    pieces = []
    for dy in range(slots):
        for dx in range(3):
            piece = ref[row + dy * step, col + dx * step : col + dx * step + n]
            pieces.append(piece.reshape(n * 16, piece.shape[-1]))
    return jnp.concatenate(pieces, 1)


def pair_weights(w_ref, out_ref, back):
    zero = jnp.zeros((MID, MID), BF16)
    for dy in range(4):
        for dx in range(3):
            for side in range(2):
                ky, kx = (2 - dy + side, 2 - dx) if back else (dy - side, dx)
                tap = zero
                if 0 <= ky < 3:
                    at = (3 * ky + kx) * MID
                    tap = w_ref[:, at : at + MID]
                    if not back:
                        tap = tap.astype(F32).T.astype(BF16)
                at = (3 * dy + dx) * MID
                out_ref[at : at + MID, side * MID : (side + 1) * MID] = tap


def weights_kernel(w4_ref, w8_ref, w4t_ref, w8t_ref, w4s_ref, w8s_ref):
    pair_weights(w4_ref, w4t_ref, False)
    pair_weights(w8_ref, w8t_ref, False)
    pair_weights(w4_ref, w4s_ref, True)
    pair_weights(w8_ref, w8s_ref, True)


def inside(pos_ref, row, col, n, rb, cb):
    rows = pos_ref[0] * rb + row
    cols = pos_ref[1] * cb + col + lax.broadcasted_iota(jnp.int32, (n * 16, 1), 0) // 16
    rows = jnp.broadcast_to(rows, cols.shape)
    return (rows >= 0) & (rows < pos_ref[2]) & (cols >= 0) & (cols < pos_ref[3])


def fill(pad_ref, own_ref, halo_refs):
    rb, cb = own_ref.shape[0], own_ref.shape[1]

    def span(step, size):
        return slice(H, H + size) if step == 0 else slice(0, H) if step > 0 else slice(H + size, None)

    pad_ref[H : H + rb, H : H + cb] = own_ref[...]
    for ref, (dr, dc) in zip(halo_refs, SIDES):
        pad_ref[span(dr, rb), span(dc, cb)] = ref[...]


def forward_kernel(pos_ref, own_ref, w4t_ref, w8t_ref, wc_ref, labels_ref, *refs):
    halo_refs, refs = refs[: len(SIDES)], refs[len(SIDES) :]
    g3_ref, h1_ref, h2_ref, slope2_ref, gc_ref = refs[:5]
    edge_refs = refs[5:]
    rb, cb = own_ref.shape[0], own_ref.shape[1]
    fill(h1_ref, own_ref, halo_refs)
    n = cb + 4

    def first(j, carry):
        both = jnp.dot(taps(h1_ref, 2 * j, 1, 0, n, 4), w4t_ref[...], preferred_element_type=F32)
        for side in range(2):
            i = 2 * j + side
            a = both[:, side * MID : (side + 1) * MID]
            s = sigmoid(a)
            h = jnp.where(inside(pos_ref, i - 2, -2, n, rb, cb), a * s, 0.0)
            h2_ref[i] = h.astype(BF16).reshape(n, 16, MID)
            slope2_ref[i] = (s * (1.0 + a * (1.0 - s))).reshape(n, 16, MID)
        return carry

    lax.fori_loop(0, (rb + 4) // 2, first, 0)
    gc_ref[...] = jnp.zeros_like(gc_ref)
    px = cb * 16
    wc = wc_ref[...]
    classes = wc.shape[0]
    for start in range(0, rb, 4):
        for j in (start, start + 1):
            both = jnp.dot(taps(h2_ref, j, 2, 0, cb, 4), w8t_ref[...], preferred_element_type=F32)
            for side in range(2):
                i = j + 2 * side
                a = both[:, side * MID : (side + 1) * MID]
                s = sigmoid(a)
                h3 = (a * s).astype(BF16)
                expo = jnp.exp(dot(wc, h3, 1, 1))
                prob = expo / jnp.sum(expo, axis=0, keepdims=True)
                label = labels_ref[:, i * px : (i + 1) * px]
                hot = (label == lax.broadcasted_iota(jnp.int32, (classes, px), 0)).astype(F32)
                g4 = (loss_weight * (prob - hot)).astype(BF16)
                gc_ref[...] += jnp.dot(g4, h3, preferred_element_type=F32)
                back = dot(g4, wc, 0, 0)
                g3 = (back * (s * (1.0 + a * (1.0 - s)))).astype(BF16).reshape(cb, 16, MID)
                g3_ref[i] = g3
                put_edges(edge_refs, i, g3, rb)


def dilate8_kernel(g3_ref, h2_ref, out_ref, acc_ref):
    rb, cb = g3_ref.shape[0], g3_ref.shape[1]
    for i in range(rb):
        g = g3_ref[i].reshape(cb * 16, MID)
        part = dot(g, taps(h2_ref, i, 2, 0, cb), 0, 0)
        if i == 0:
            acc_ref[...] = part
        else:
            acc_ref[...] += part
    for t in range(9):
        out_ref[t * MID : (t + 1) * MID, :] = acc_ref[:, t * MID : (t + 1) * MID].astype(BF16)


def backward_kernel(pos_ref, own_ref, w4s_ref, w8s_ref, h1_ref, slope2_ref, a1_ref, *refs):
    halo_refs = refs[: len(SIDES)]
    g1_ref, out_ref, g3_ref, g2_ref, acc_ref = refs[len(SIDES) :]
    rb, cb = own_ref.shape[0], own_ref.shape[1]
    cols = cb * B
    fill(g3_ref, own_ref, halo_refs)
    n = cb + 2

    def second(back, i):
        g = back * slope2_ref[i + 1, 1 : 1 + n].reshape(n * 16, MID)
        g = jnp.where(inside(pos_ref, i - 1, -1, n, rb, cb), g, 0.0)
        g2_ref[i] = g.astype(BF16).reshape(n, 16, MID)

    for i in range(0, rb + 2, 4):
        for j in range(i, min(i + 2, rb + 2)):
            if j + 2 < rb + 2:
                both = jnp.dot(taps(g3_ref, j, 2, 0, n, 4), w8s_ref[...], preferred_element_type=F32)
                second(both[:, :MID], j)
                second(both[:, MID:], j + 2)
            else:
                one = w8s_ref[: 9 * MID, :MID]
                second(jnp.dot(taps(g3_ref, j, 2, 0, n), one, preferred_element_type=F32), j)
    for j in range(0, rb, 2):
        both = jnp.dot(taps(g2_ref, j, 1, 0, cb, 4), w4s_ref[...], preferred_element_type=F32)
        for side in range(2):
            i = j + side
            g = g2_ref[i + 1, 1 : 1 + cb].reshape(cb * 16, MID)
            part = dot(g, taps(h1_ref, i + 2, 1, 2, cb), 0, 0)
            if i == 0:
                acc_ref[...] = part
            else:
                acc_ref[...] += part
            back = both[:, side * MID : (side + 1) * MID]
            for r, row in enumerate(from_blocks(back.reshape(cb, 16, MID))):
                at = (i * B + r) * cols
                a = a1_ref[:, at : at + cols]
                s = sigmoid(a)
                g1_ref[:, at : at + cols] = (row.T * (s * (1.0 + a * (1.0 - s)))).astype(BF16)
    for t in range(9):
        out_ref[t * MID : (t + 1) * MID, :] = acc_ref[:, t * MID : (t + 1) * MID].astype(BF16)


def spans(start, count, length):
    while count:
        group, offset = divmod(start, length)
        size = min(count, length - offset)
        yield group, offset, size
        start, count = start + size, count - size


def pack_kernel(length, gi_ref, g4_ref, g8_ref, gc_ref, out_ref):
    groups = out_ref.shape[0]

    def put(at, value):
        done = 0
        for group, offset, size in spans(at, value.shape[0], length):
            out_ref[group, offset : offset + size, :] = value[done : done + size]
            done += size
        return at + done

    at = 0
    for t in range(gi_ref.shape[1] // MID):
        at = put(at, gi_ref[:, t * MID : (t + 1) * MID].astype(BF16))
    for ref in (g4_ref, g8_ref, gc_ref):
        at = put(at, ref[...].astype(BF16))
    put(at, jnp.zeros((groups * length - at, MID), BF16))
    for group in range(groups):
        out_ref[group, length:, :] = jnp.zeros((out_ref.shape[1] - length, MID), BF16)


def unpack_kernel(part_ref, gi_ref, g4_ref, g8_ref, gc_ref):
    length = part_ref.shape[1]

    def piece(at, count):
        got = [
            part_ref[group, offset : offset + size, :].astype(F32)
            for group, offset, size in spans(at, count, length)
        ]
        return got[0] if len(got) == 1 else jnp.concatenate(got, 0)

    at = 0
    for ref in (gi_ref, g4_ref, g8_ref):
        for t in range(ref.shape[1] // MID):
            ref[:, t * MID : (t + 1) * MID] = piece(at, MID)
            at += MID
    gc_ref[...] = piece(at, gc_ref.shape[0])


ROWS, COLS = ("x", "z"), ("y", "c")
PLANE = ("z", "x")


def halos(edges):
    rows, cols = lax.axis_size(ROWS), lax.axis_size(COLS)
    got = []
    for edge, (dr, dc) in zip(edges, SIDES):
        pairs = [
            (i * cols + j, (i + dr) * cols + j + dc)
            for i in range(rows) for j in range(cols)
            if 0 <= i + dr < rows and 0 <= j + dc < cols
        ]
        got.append(lax.ppermute(edge, ROWS + COLS, pairs))
    return got


def over_devices(packed, length):
    cores, ys, plane = lax.axis_size("c"), lax.axis_size("y"), lax.axis_size(PLANE)

    def exchange(v, axes, n):
        v = lax.all_to_all(v.reshape(n, -1, MID), axes, 0, 0, tiled=True)
        return jnp.sum(v.astype(F32), 0).astype(BF16)

    part = exchange(packed, "c", cores)
    part = exchange(part, ("y",) + PLANE, ys * plane)
    part = jnp.broadcast_to(part[None], (ys * plane,) + part.shape)
    part = lax.all_to_all(part, ("y",) + PLANE, 0, 0, tiled=True)
    part = part.reshape(ys, -1, MID)[:, :length].reshape(-1, MID)
    return lax.all_gather(part, "c", axis=0, tiled=True).reshape(cores * ys, length, MID)


def local(features, labels, w_input, w_dilate4, w_dilate8, w_classes):
    chans, rows, cols = features.shape
    rb, cb = rows // B, cols // B
    px = rows * cols
    classes = w_classes.shape[0]
    conv = 2 * 9 * MID * MID * px

    pos = jnp.stack([
        lax.axis_index(ROWS), lax.axis_index(COLS),
        jnp.int32(rb * lax.axis_size(ROWS)), jnp.int32(cb * lax.axis_size(COLS)),
    ]).astype(jnp.int32)
    order = labels.reshape(rb, B, cb, B).transpose(0, 2, 1, 3).reshape(1, px)

    a1 = jnp.dot(w_input, features.reshape(chans, px), preferred_element_type=F32)
    tile = ((rb, cb, 16, MID), BF16)
    edges = edge_shapes(rb, cb)
    h1, *sent = call(squeeze_kernel, "squeeze", [tile] + edges, 1, flops=px * MID)(a1)
    around = halos(sent)

    padded = ((rb + 2 * H, cb + 2 * H, 16, MID), BF16)
    weight = ((12 * MID, 2 * MID), BF16)
    w4t, w8t, w4s, w8s = call(weights_kernel, "weights", [weight] * 4, 2, flops=conv // 4)(w_dilate4, w_dilate8)
    g3, h1_pad, h2_pad, slope2, gc, *sent = call(
        forward_kernel, "forward",
        [tile, padded, ((rb + 4, cb + 4, 16, MID), BF16), ((rb + 4, cb + 4, 16, MID), F32),
         ((classes, MID), F32)] + edges,
        6 + len(SIDES), flops=4 * conv, smem=1,
    )(pos, h1, w4t, w8t, w_classes, order, *around)
    around = halos(sent)
    acc = pltpu.VMEM((MID, 9 * MID), F32)
    (g8,) = call(dilate8_kernel, "dilate8", [((9 * MID, MID), BF16)], 2, [acc], flops=conv)(g3, h2_pad)
    g1, g4 = call(
        backward_kernel, "backward",
        [((MID, px), BF16), ((9 * MID, MID), BF16)],
        7 + len(SIDES),
        [pltpu.VMEM(*padded), pltpu.VMEM((rb + 2, cb + 2, 16, MID), BF16), acc],
        flops=4 * conv, smem=1,
    )(pos, g3, w4s, w8s, h1_pad, slope2, a1, *around)
    gi = lax.dot_general(
        g1.reshape(MID, rows, cols), features, (((1, 2), (1, 2)), ((), ())), preferred_element_type=F32
    )

    used = MID * (chans // MID + 18) + classes
    groups = lax.axis_size(COLS)
    length = -(-used // (16 * groups)) * 16
    unit = -(-length // (8 * lax.axis_size(PLANE))) * 8
    (packed,) = call(
        lambda *refs: pack_kernel(length, *refs), "pack",
        [((groups, unit * lax.axis_size(PLANE), MID), BF16)], 4,
    )(gi, g4, g8, gc)
    part = over_devices(packed, length)
    return tuple(call(
        unpack_kernel, "unpack",
        [((MID, chans), F32), ((MID, 9 * MID), F32), ((MID, 9 * MID), F32), ((classes, MID), F32)], 1,
    )(part))


def solution(mesh):
    rows, cols = mesh.shape["rows"], mesh.shape["cols"]
    inner = math.gcd(rows, 8)
    torus = Mesh(mesh.devices.reshape(rows // inner, inner, cols // 2, 2), ROWS + COLS)
    return jax.shard_map(
        local,
        mesh=torus,
        in_specs=(P(None, ROWS, COLS), P(ROWS, COLS), P(), P(), P(), P()),
        out_specs=(P(), P(), P(), P()),
        check_vma=False,
    )
```

```python
import math

import jax
import jax.numpy as jnp
from jax import lax
from jax.experimental import pallas as pl
from jax.experimental.pallas import tpu as pltpu
from jax.sharding import Mesh, PartitionSpec as P

loss_weight = 0.03125
B = 4
H = 3
MID = 128
SIDES = ((1, 0), (-1, 0), (0, 1), (0, -1))
F32 = jnp.float32
BF16 = jnp.bfloat16


def vmem(n):
    return [pl.BlockSpec(memory_space=pltpu.VMEM)] * n


def call(body, name, outs, n_in, scratch=(), flops=0, smem=0, limit=20 << 20):
    shapes = [jax.ShapeDtypeStruct(s, d) for s, d in outs]
    size = sum(math.prod(s) * jnp.dtype(d).itemsize for s, d in outs)
    return pl.pallas_call(
        body,
        name=name,
        out_shape=shapes,
        in_specs=[pl.BlockSpec(memory_space=pltpu.SMEM)] * smem + vmem(n_in - smem),
        out_specs=vmem(len(outs)),
        scratch_shapes=list(scratch),
        compiler_params=pltpu.CompilerParams(vmem_limit_bytes=limit),
        cost_estimate=pl.CostEstimate(flops=flops, bytes_accessed=2 * size, transcendentals=0),
    )


def to_blocks(rows):
    cols, ch = rows[0].shape
    sub = lax.broadcasted_iota(jnp.int32, (cols // 8, 8, ch), 1)

    def pair(low, high):
        low, high = low.reshape(cols // 8, 8, ch), high.reshape(cols // 8, 8, ch)
        even = jnp.where(sub < 4, low, pltpu.roll(high, 4, 1))
        odd = jnp.where(sub < 4, pltpu.roll(low, 4, 1), high)
        return jnp.stack([even, odd], 1).reshape(cols // 4, 8, ch)

    return jnp.concatenate([pair(rows[0], rows[1]), pair(rows[2], rows[3])], 1)


def from_blocks(tile):
    blocks, _, ch = tile.shape
    sub = lax.broadcasted_iota(jnp.int32, (blocks // 2, 8, ch), 1)
    rows = []
    for half in range(2):
        v = tile[:, half * 8 : half * 8 + 8, :].reshape(blocks // 2, 2, 8, ch)
        even, odd = v[:, 0], v[:, 1]
        low = jnp.where(sub < 4, even, pltpu.roll(odd, 4, 1))
        high = jnp.where(sub < 4, pltpu.roll(even, 4, 1), odd)
        rows += [low.reshape(blocks * 4, ch), high.reshape(blocks * 4, ch)]
    return rows


def sigmoid(a):
    return 1.0 / (1.0 + jnp.exp(-a))


def dot(a, b, ca, cb):
    return lax.dot_general(a, b, (((ca,), (cb,)), ((), ())), preferred_element_type=F32)


def edge_shapes(rb, cb):
    return [((H if dr else rb, H if dc else cb, 16, MID), BF16) for dr, dc in SIDES]


def put_edges(refs, i, row, rb):
    cb = row.shape[0]
    for ref, (dr, dc) in zip(refs, SIDES):
        piece = row[:H] if dc < 0 else row[cb - H :] if dc > 0 else row
        if dr == 0:
            ref[i] = piece
        elif dr < 0 and i < H:
            ref[i] = piece
        elif dr > 0 and i >= rb - H:
            ref[i - (rb - H)] = piece


def squeeze_kernel(a1_ref, h1_ref, *edge_refs):
    rb, cb = h1_ref.shape[0], h1_ref.shape[1]
    cols = cb * B
    for i in range(rb):
        rows = [a1_ref[:, (i * B + r) * cols : (i * B + r + 1) * cols].T for r in range(B)]
        a = to_blocks(rows)
        h = (a * sigmoid(a)).astype(BF16)
        h1_ref[i] = h
        put_edges(edge_refs, i, h, rb)


def taps(ref, row, step, col, n, slots=3):
    pieces = []
    for dy in range(slots):
        for dx in range(3):
            piece = ref[row + dy * step, col + dx * step : col + dx * step + n]
            pieces.append(piece.reshape(n * 16, piece.shape[-1]))
    return jnp.concatenate(pieces, 1)


def pair_weights(w_ref, out_ref, back):
    zero = jnp.zeros((MID, MID), BF16)
    for dy in range(4):
        for dx in range(3):
            for side in range(2):
                ky, kx = (2 - dy + side, 2 - dx) if back else (dy - side, dx)
                tap = zero
                if 0 <= ky < 3:
                    at = (3 * ky + kx) * MID
                    tap = w_ref[:, at : at + MID]
                    if not back:
                        tap = tap.astype(F32).T.astype(BF16)
                at = (3 * dy + dx) * MID
                out_ref[at : at + MID, side * MID : (side + 1) * MID] = tap


def weights_kernel(w4_ref, w8_ref, w4t_ref, w8t_ref, w4s_ref, w8s_ref):
    pair_weights(w4_ref, w4t_ref, False)
    pair_weights(w8_ref, w8t_ref, False)
    pair_weights(w4_ref, w4s_ref, True)
    pair_weights(w8_ref, w8s_ref, True)


def inside(pos_ref, row, col, n, rb, cb):
    rows = pos_ref[0] * rb + row
    cols = pos_ref[1] * cb + col + lax.broadcasted_iota(jnp.int32, (n * 16, 1), 0) // 16
    rows = jnp.broadcast_to(rows, cols.shape)
    return (rows >= 0) & (rows < pos_ref[2]) & (cols >= 0) & (cols < pos_ref[3])


def fill(pad_ref, own_ref, halo_refs):
    rb, cb = own_ref.shape[0], own_ref.shape[1]
    up_ref, down_ref, left_ref, right_ref = halo_refs
    pad_ref[:H, H : H + cb] = up_ref[...]
    pad_ref[H : H + rb, H : H + cb] = own_ref[...]
    pad_ref[H + rb :, H : H + cb] = down_ref[...]
    pad_ref[:, :H] = left_ref[...]
    pad_ref[:, H + cb :] = right_ref[...]


def forward_kernel(pos_ref, own_ref, w4t_ref, w8t_ref, wc_ref, labels_ref, *refs):
    halo_refs, refs = refs[: len(SIDES)], refs[len(SIDES) :]
    g3_ref, h1_ref, h2_ref, slope2_ref, gc_ref = refs[:5]
    edge_refs = refs[5:]
    rb, cb = own_ref.shape[0], own_ref.shape[1]
    fill(h1_ref, own_ref, halo_refs)
    n = cb + 4

    def first(j, carry):
        both = jnp.dot(taps(h1_ref, 2 * j, 1, 0, n, 4), w4t_ref[...], preferred_element_type=F32)
        for side in range(2):
            i = 2 * j + side
            a = both[:, side * MID : (side + 1) * MID]
            s = sigmoid(a)
            h = jnp.where(inside(pos_ref, i - 2, -2, n, rb, cb), a * s, 0.0)
            h2_ref[i] = h.astype(BF16).reshape(n, 16, MID)
            slope2_ref[i] = (s * (1.0 + a * (1.0 - s))).reshape(n, 16, MID)
        return carry

    lax.fori_loop(0, (rb + 4) // 2, first, 0)
    gc_ref[...] = jnp.zeros_like(gc_ref)
    px = cb * 16
    wc = wc_ref[...]
    classes = wc.shape[0]
    for start in range(0, rb, 4):
        for j in (start, start + 1):
            both = jnp.dot(taps(h2_ref, j, 2, 0, cb, 4), w8t_ref[...], preferred_element_type=F32)
            for side in range(2):
                i = j + 2 * side
                a = both[:, side * MID : (side + 1) * MID]
                s = sigmoid(a)
                h3 = (a * s).astype(BF16)
                expo = jnp.exp(dot(wc, h3, 1, 1))
                prob = expo / jnp.sum(expo, axis=0, keepdims=True)
                label = labels_ref[:, i * px : (i + 1) * px]
                hot = (label == lax.broadcasted_iota(jnp.int32, (classes, px), 0)).astype(F32)
                g4 = (loss_weight * (prob - hot)).astype(BF16)
                gc_ref[...] += jnp.dot(g4, h3, preferred_element_type=F32)
                back = dot(g4, wc, 0, 0)
                g3 = (back * (s * (1.0 + a * (1.0 - s)))).astype(BF16).reshape(cb, 16, MID)
                g3_ref[i] = g3
                put_edges(edge_refs, i, g3, rb)


def dilate8_kernel(g3_ref, h2_ref, out_ref, acc_ref):
    rb, cb = g3_ref.shape[0], g3_ref.shape[1]
    for i in range(rb):
        g = g3_ref[i].reshape(cb * 16, MID)
        part = dot(g, taps(h2_ref, i, 2, 0, cb), 0, 0)
        if i == 0:
            acc_ref[...] = part
        else:
            acc_ref[...] += part
    for t in range(9):
        out_ref[t * MID : (t + 1) * MID, :] = acc_ref[:, t * MID : (t + 1) * MID].astype(BF16)


def backward_kernel(pos_ref, own_ref, w4s_ref, w8s_ref, h1_ref, slope2_ref, a1_ref, *refs):
    halo_refs = refs[: len(SIDES)]
    g1_ref, out_ref, g3_ref, g2_ref, acc_ref = refs[len(SIDES) :]
    rb, cb = own_ref.shape[0], own_ref.shape[1]
    cols = cb * B
    fill(g3_ref, own_ref, halo_refs)
    n = cb + 2

    def second(back, i):
        g = back * slope2_ref[i + 1, 1 : 1 + n].reshape(n * 16, MID)
        g = jnp.where(inside(pos_ref, i - 1, -1, n, rb, cb), g, 0.0)
        g2_ref[i] = g.astype(BF16).reshape(n, 16, MID)

    for i in range(0, rb + 2, 4):
        for j in range(i, min(i + 2, rb + 2)):
            if j + 2 < rb + 2:
                both = jnp.dot(taps(g3_ref, j, 2, 0, n, 4), w8s_ref[...], preferred_element_type=F32)
                second(both[:, :MID], j)
                second(both[:, MID:], j + 2)
            else:
                one = w8s_ref[: 9 * MID, :MID]
                second(jnp.dot(taps(g3_ref, j, 2, 0, n), one, preferred_element_type=F32), j)
    for j in range(0, rb, 2):
        both = jnp.dot(taps(g2_ref, j, 1, 0, cb, 4), w4s_ref[...], preferred_element_type=F32)
        for side in range(2):
            i = j + side
            g = g2_ref[i + 1, 1 : 1 + cb].reshape(cb * 16, MID)
            part = dot(g, taps(h1_ref, i + 2, 1, 2, cb), 0, 0)
            if i == 0:
                acc_ref[...] = part
            else:
                acc_ref[...] += part
            back = both[:, side * MID : (side + 1) * MID]
            for r, row in enumerate(from_blocks(back.reshape(cb, 16, MID))):
                at = (i * B + r) * cols
                a = a1_ref[:, at : at + cols]
                s = sigmoid(a)
                g1_ref[:, at : at + cols] = (row.T * (s * (1.0 + a * (1.0 - s)))).astype(BF16)
    for t in range(9):
        out_ref[t * MID : (t + 1) * MID, :] = acc_ref[:, t * MID : (t + 1) * MID].astype(BF16)


def spans(start, count, length):
    while count:
        group, offset = divmod(start, length)
        size = min(count, length - offset)
        yield group, offset, size
        start, count = start + size, count - size


def pack_kernel(length, cores, gi_ref, g4_ref, g8_ref, gc_ref, out_ref):
    groups = out_ref.shape[0]

    def put(at, value):
        done = 0
        for group, offset, size in spans(at, value.shape[0], length):
            out_ref[group, offset : offset + size, :] = value[done : done + size]
            done += size
        return at + done

    at = 0
    for t in range(gi_ref.shape[1] // MID):
        at = put(at, gi_ref[:, t * MID : (t + 1) * MID].astype(BF16))
    for ref in (g4_ref, g8_ref):
        at = put(at, ref[...])
    if at < groups * length:
        put(at, jnp.zeros((groups * length - at, MID), BF16))
    half = gc_ref.shape[0] // cores
    for group in range(groups):
        core = group // (groups // cores)
        out_ref[group, length:, :] = gc_ref[core * half : (core + 1) * half, :].astype(BF16)


def unpack_kernel(part_ref, gi_ref, g4_ref, g8_ref, gc_ref):
    cores = part_ref.shape[0]
    half = gc_ref.shape[0] // cores
    length = part_ref.shape[1] - half

    def piece(at, count):
        got = [
            part_ref[core, offset : offset + size, :].astype(F32)
            for core, offset, size in spans(at, count, length)
        ]
        return got[0] if len(got) == 1 else jnp.concatenate(got, 0)

    at = 0
    for ref in (gi_ref, g4_ref, g8_ref):
        for t in range(ref.shape[1] // MID):
            ref[:, t * MID : (t + 1) * MID] = piece(at, MID)
            at += MID
    for core in range(cores):
        gc_ref[core * half : (core + 1) * half, :] = part_ref[core, length:, :].astype(F32)


ROWS, COLS = ("x", "z"), ("y", "c")
PLANE = ("z", "x")


def neighbour(value, axes, step):
    count = lax.axis_size(axes)
    pairs = [(i, i + step) for i in range(count) if 0 <= i + step < count]
    return lax.ppermute(value, axes, pairs)


def halos(edges, beside):
    bottom, top, right, left = edges
    up = neighbour(bottom, ROWS, 1)
    down = neighbour(top, ROWS, -1)
    right, left, beside = lax.optimization_barrier((right, left, beside))
    cb = up.shape[1]
    east = jnp.concatenate([up[:, cb - H :], right, down[:, cb - H :]], 0)
    west = jnp.concatenate([up[:, :H], left, down[:, :H]], 0)
    return (up, down, neighbour(east, COLS, 1), neighbour(west, COLS, -1)), beside


def over_devices(packed, length):
    cores, ys, plane = lax.axis_size("c"), lax.axis_size("y"), lax.axis_size(PLANE)

    def swap(v, axes):
        return lax.all_to_all(v, axes, 0, 0, tiled=True)

    def total(v):
        return jnp.sum(v.astype(F32), 0).astype(BF16)

    def copies(v, n):
        return jnp.broadcast_to(v[None], (n,) + v.shape)

    part = total(swap(packed.reshape(cores, -1, MID), "c"))
    part = total(swap(part.reshape(plane, -1, MID), PLANE))
    part = total(swap(copies(part, ys), "y"))
    whole = swap(copies(part[:length], plane), PLANE).reshape(-1, MID)
    whole = jnp.concatenate([whole, part[length:]], 0)
    return lax.all_gather(whole, "c", axis=0, tiled=True).reshape(cores, -1, MID)


def local(features, labels, w_input, w_dilate4, w_dilate8, w_classes):
    chans, rows, cols = features.shape
    rb, cb = rows // B, cols // B
    px = rows * cols
    classes = w_classes.shape[0]
    conv = 2 * 9 * MID * MID * px

    pos = jnp.stack([
        lax.axis_index(ROWS), lax.axis_index(COLS),
        jnp.int32(rb * lax.axis_size(ROWS)), jnp.int32(cb * lax.axis_size(COLS)),
    ]).astype(jnp.int32)
    order = labels.reshape(rb, B, cb, B).transpose(0, 2, 1, 3).reshape(1, px)

    a1 = jnp.dot(w_input, features.reshape(chans, px), preferred_element_type=F32)
    tile = ((rb, cb, 16, MID), BF16)
    edges = edge_shapes(rb, cb)
    h1, *sent = call(squeeze_kernel, "squeeze", [tile] + edges, 1, flops=px * MID)(a1)
    padded = ((rb + 2 * H, cb + 2 * H, 16, MID), BF16)
    weight = ((12 * MID, 2 * MID), BF16)
    weights = call(weights_kernel, "weights", [weight] * 4, 2, flops=conv // 4)(w_dilate4, w_dilate8)
    around, ((w4t, w8t, w4s, w8s), order, pos) = halos(sent, (weights, order, pos))
    g3, h1_pad, h2_pad, slope2, gc, *sent = call(
        forward_kernel, "forward",
        [tile, padded, ((rb + 4, cb + 4, 16, MID), BF16), ((rb + 4, cb + 4, 16, MID), F32),
         ((classes, MID), F32)] + edges,
        6 + len(SIDES), flops=4 * conv, smem=1,
    )(pos, h1, w4t, w8t, w_classes, order, *around)
    acc = pltpu.VMEM((MID, 9 * MID), F32)
    (g8,) = call(dilate8_kernel, "dilate8", [((9 * MID, MID), BF16)], 2, [acc], flops=conv)(g3, h2_pad)
    around, g8 = halos(sent, g8)
    g1, g4 = call(
        backward_kernel, "backward",
        [((MID, px), BF16), ((9 * MID, MID), BF16)],
        7 + len(SIDES),
        [pltpu.VMEM(*padded), pltpu.VMEM((rb + 2, cb + 2, 16, MID), BF16), acc],
        flops=4 * conv, smem=1,
    )(pos, g3, w4s, w8s, h1_pad, slope2, a1, *around)
    gi = lax.dot_general(
        g1.reshape(MID, rows, cols), features, (((1, 2), (1, 2)), ((), ())), preferred_element_type=F32
    )

    cores, plane = lax.axis_size("c"), lax.axis_size(PLANE)
    length = -(-MID * (chans // MID + 18) // (8 * cores * plane)) * 8
    (packed,) = call(
        lambda *refs: pack_kernel(length, cores, *refs), "pack",
        [((cores * plane, length + classes // cores, MID), BF16)], 4,
    )(gi, g4, g8, gc)
    part = over_devices(packed, length)
    return tuple(call(
        unpack_kernel, "unpack",
        [((MID, chans), F32), ((MID, 9 * MID), F32), ((MID, 9 * MID), F32), ((classes, MID), F32)], 1,
    )(part))


def solution(mesh):
    rows, cols = mesh.shape["rows"], mesh.shape["cols"]
    inner = math.gcd(rows, 8)
    torus = Mesh(mesh.devices.reshape(rows // inner, inner, cols // 2, 2), ROWS + COLS)
    return jax.shard_map(
        local,
        mesh=torus,
        in_specs=(P(None, ROWS, COLS), P(ROWS, COLS), P(), P(), P(), P()),
        out_specs=(P(), P(), P(), P()),
        check_vma=False,
    )
```

```python
import math

import jax
import jax.numpy as jnp
from jax import lax
from jax.experimental import pallas as pl
from jax.experimental.pallas import tpu as pltpu
from jax.sharding import Mesh, PartitionSpec as P

loss_weight = 0.03125
B = 4
H = 3
MID = 128
SIDES = ((1, 0), (-1, 0), (0, 1), (0, -1))
UNROLL = 4
ROWS, COLS = ("x", "z"), ("y", "c")
PLANE = ("z", "x")
F32 = jnp.float32
BF16 = jnp.bfloat16


def vmem(n):
    return [pl.BlockSpec(memory_space=pltpu.VMEM)] * n


def call(body, name, outs, n_in, scratch=(), flops=0, limit=10 << 20):
    shapes = [jax.ShapeDtypeStruct(s, d) for s, d in outs]
    size = sum(math.prod(s) * jnp.dtype(d).itemsize for s, d in outs)
    return pl.pallas_call(
        body,
        name=name,
        out_shape=shapes,
        in_specs=vmem(n_in),
        out_specs=vmem(len(outs)),
        scratch_shapes=list(scratch),
        compiler_params=pltpu.CompilerParams(vmem_limit_bytes=limit),
        cost_estimate=pl.CostEstimate(flops=flops, bytes_accessed=2 * size, transcendentals=0),
    )


def to_blocks(rows):
    cols, ch = rows[0].shape
    sub = lax.broadcasted_iota(jnp.int32, (cols // 8, 8, ch), 1)

    def pair(low, high):
        low, high = low.reshape(cols // 8, 8, ch), high.reshape(cols // 8, 8, ch)
        even = jnp.where(sub < 4, low, pltpu.roll(high, 4, 1))
        odd = jnp.where(sub < 4, pltpu.roll(low, 4, 1), high)
        return jnp.stack([even, odd], 1).reshape(cols // 4, 8, ch)

    return jnp.concatenate([pair(rows[0], rows[1]), pair(rows[2], rows[3])], 1)


def from_blocks(tile):
    blocks, _, ch = tile.shape
    sub = lax.broadcasted_iota(jnp.int32, (blocks // 2, 8, ch), 1)
    rows = []
    for half in range(2):
        v = tile[:, half * 8 : half * 8 + 8, :].reshape(blocks // 2, 2, 8, ch)
        even, odd = v[:, 0], v[:, 1]
        low = jnp.where(sub < 4, even, pltpu.roll(odd, 4, 1))
        high = jnp.where(sub < 4, pltpu.roll(even, 4, 1), odd)
        rows += [low.reshape(blocks * 4, ch), high.reshape(blocks * 4, ch)]
    return rows


def sigmoid(a):
    return 0.5 + 0.5 * jnp.tanh(0.5 * a)


def smooth(a):
    s = sigmoid(a)
    h = a * s
    return h, s + h * (1.0 - s)


def dot(a, b, ca, cb):
    return lax.dot_general(a, b, (((ca,), (cb,)), ((), ())), preferred_element_type=F32)


def edge_shapes(rb, cb):
    return [((H if dr else rb, H if dc else cb, 16, MID), BF16) for dr, dc in SIDES]


def put_edges(refs, i, row, rb):
    cb = row.shape[0]
    for ref, (dr, dc) in zip(refs, SIDES):
        piece = row[:H] if dc < 0 else row[cb - H :] if dc > 0 else row
        if dr == 0:
            ref[i] = piece
        elif dr < 0 and i < H:
            ref[i] = piece
        elif dr > 0 and i >= rb - H:
            ref[i - (rb - H)] = piece


def squeeze_kernel(a1_ref, h1_ref, *edge_refs):
    rb, cb = h1_ref.shape[0], h1_ref.shape[1]
    cols = cb * B
    for i in range(rb):
        rows = [a1_ref[:, (i * B + r) * cols : (i * B + r + 1) * cols].T for r in range(B)]
        a = to_blocks(rows)
        h = (a * sigmoid(a)).astype(BF16)
        h1_ref[i] = h
        put_edges(edge_refs, i, h, rb)


def taps(ref, row, step, col, n, slots=3):
    pieces = []
    for dy in range(slots):
        for dx in range(3):
            piece = ref[row + dy * step, col + dx * step : col + dx * step + n]
            pieces.append(piece.reshape(n * 16, piece.shape[-1]))
    return jnp.concatenate(pieces, 1)


def pair_weights(w_ref, out_ref, back):
    zero = jnp.zeros((MID, MID), BF16)
    for dy in range(4):
        for dx in range(3):
            for side in range(2):
                ky, kx = (2 - dy + side, 2 - dx) if back else (dy - side, dx)
                tap = zero
                if 0 <= ky < 3:
                    at = (3 * ky + kx) * MID
                    tap = w_ref[:, at : at + MID]
                    if not back:
                        tap = tap.astype(F32).T.astype(BF16)
                at = (3 * dy + dx) * MID
                out_ref[at : at + MID, side * MID : (side + 1) * MID] = tap


def prepare_kernel(w4_ref, w8_ref, labels_ref, w4t_ref, w8t_ref, w4s_ref, w8s_ref, order_ref):
    pair_weights(w4_ref, w4t_ref, False)
    pair_weights(w8_ref, w8t_ref, False)
    pair_weights(w4_ref, w4s_ref, True)
    pair_weights(w8_ref, w8s_ref, True)
    rows, cols = labels_ref.shape
    labels = labels_ref[...].astype(F32).T
    px = cols * B
    for i in range(rows // B):
        wide = [jnp.broadcast_to(labels[:, y : y + 1], (cols, MID)) for y in range(i * B, i * B + B)]
        order_ref[:, i * px : (i + 1) * px] = to_blocks(wide).reshape(px, MID).T[:1]


def place(axes):
    index, size = 0, 1
    for axis in axes:
        index = index * lax.axis_size(axis) + lax.axis_index(axis)
        size = size * lax.axis_size(axis)
    return index, size


def clear_outside(ref, reach):
    row, rows = place(ROWS)
    col, cols = place(COLS)

    @pl.when(row == 0)
    def _():
        ref[:reach] = jnp.zeros((reach,) + ref.shape[1:], ref.dtype)

    @pl.when(row == rows - 1)
    def _():
        ref[ref.shape[0] - reach :] = jnp.zeros((reach,) + ref.shape[1:], ref.dtype)

    side = jnp.zeros((ref.shape[0], reach) + ref.shape[2:], ref.dtype)

    @pl.when(col == 0)
    def _():
        ref[:, :reach] = side

    @pl.when(col == cols - 1)
    def _():
        ref[:, ref.shape[1] - reach :] = side


def fill(pad_ref, own_ref, halo_refs):
    rb, cb = own_ref.shape[0], own_ref.shape[1]
    up_ref, down_ref, left_ref, right_ref = halo_refs
    pad_ref[:H, H : H + cb] = up_ref[...]
    pad_ref[H : H + rb, H : H + cb] = own_ref[...]
    pad_ref[H + rb :, H : H + cb] = down_ref[...]
    pad_ref[:, :H] = left_ref[...]
    pad_ref[:, H + cb :] = right_ref[...]


def forward_kernel(own_ref, w4t_ref, w8t_ref, wc_ref, labels_ref, *refs):
    halo_refs, refs = refs[: len(SIDES)], refs[len(SIDES) :]
    g3_ref, h1_ref, h2_ref, slope2_ref, gc_ref = refs[:5]
    edge_refs = refs[5:]
    rb, cb = own_ref.shape[0], own_ref.shape[1]
    fill(h1_ref, own_ref, halo_refs)
    n = cb + 4

    def first(j, carry):
        both = jnp.dot(taps(h1_ref, 2 * j, 1, 0, n, 4), w4t_ref[...], preferred_element_type=F32)
        for side in range(2):
            i = 2 * j + side
            h, slope = smooth(both[:, side * MID : (side + 1) * MID])
            h2_ref[i] = h.astype(BF16).reshape(n, 16, MID)
            slope2_ref[i] = slope.reshape(n, 16, MID)
        return carry

    lax.fori_loop(0, (rb + 4) // 2, first, 0, unroll=UNROLL)
    clear_outside(h2_ref, 2)
    gc_ref[...] = jnp.zeros_like(gc_ref)
    px = cb * 16
    wc = wc_ref[...]
    classes = wc.shape[0]
    for start in range(0, rb, 4):
        for j in (start, start + 1):
            both = jnp.dot(taps(h2_ref, j, 2, 0, cb, 4), w8t_ref[...], preferred_element_type=F32)
            for side in range(2):
                i = j + 2 * side
                h3, slope = smooth(both[:, side * MID : (side + 1) * MID])
                h3 = h3.astype(BF16)
                expo = jnp.exp(dot(wc, h3, 1, 1))
                prob = expo / jnp.sum(expo, axis=0, keepdims=True)
                label = labels_ref[:, i * px : (i + 1) * px]
                hot = (label == lax.broadcasted_iota(jnp.int32, (classes, px), 0).astype(F32)).astype(F32)
                g4 = (loss_weight * (prob - hot)).astype(BF16)
                gc_ref[...] += jnp.dot(g4, h3, preferred_element_type=F32)
                back = dot(g4, wc, 0, 0)
                g3 = (back * slope).astype(BF16).reshape(cb, 16, MID)
                g3_ref[i] = g3
                put_edges(edge_refs, i, g3, rb)


def dilate8_kernel(g3_ref, h2_ref, out_ref, acc_ref):
    rb, cb = g3_ref.shape[0], g3_ref.shape[1]
    for i in range(rb):
        g = g3_ref[i].reshape(cb * 16, MID)
        part = dot(g, taps(h2_ref, i, 2, 0, cb), 0, 0)
        if i == 0:
            acc_ref[...] = part
        else:
            acc_ref[...] += part
    for t in range(9):
        out_ref[t * MID : (t + 1) * MID, :] = acc_ref[:, t * MID : (t + 1) * MID].astype(BF16)


def backward_kernel(own_ref, w4s_ref, w8s_ref, h1_ref, slope2_ref, a1_ref, *refs):
    halo_refs = refs[: len(SIDES)]
    g1_ref, out_ref, g3_ref, g2_ref, acc_ref = refs[len(SIDES) :]
    rb, cb = own_ref.shape[0], own_ref.shape[1]
    cols = cb * B
    fill(g3_ref, own_ref, halo_refs)
    n = cb + 2

    def second(back, i):
        g = back * slope2_ref[i + 1, 1 : 1 + n].reshape(n * 16, MID)
        g2_ref[i] = g.astype(BF16).reshape(n, 16, MID)

    for i in range(0, rb + 2, 4):
        for j in range(i, min(i + 2, rb + 2)):
            if j + 2 < rb + 2:
                both = jnp.dot(taps(g3_ref, j, 2, 0, n, 4), w8s_ref[...], preferred_element_type=F32)
                second(both[:, :MID], j)
                second(both[:, MID:], j + 2)
            else:
                one = w8s_ref[: 9 * MID, :MID]
                second(jnp.dot(taps(g3_ref, j, 2, 0, n), one, preferred_element_type=F32), j)
    clear_outside(g2_ref, 1)
    for j in range(0, rb, 2):
        both = jnp.dot(taps(g2_ref, j, 1, 0, cb, 4), w4s_ref[...], preferred_element_type=F32)
        for side in range(2):
            i = j + side
            g = g2_ref[i + 1, 1 : 1 + cb].reshape(cb * 16, MID)
            part = dot(g, taps(h1_ref, i + 2, 1, 2, cb), 0, 0)
            if i == 0:
                acc_ref[...] = part
            else:
                acc_ref[...] += part
            back = both[:, side * MID : (side + 1) * MID]
            for r, row in enumerate(from_blocks(back.reshape(cb, 16, MID))):
                at = (i * B + r) * cols
                _, slope = smooth(a1_ref[:, at : at + cols])
                g1_ref[:, at : at + cols] = (row.T * slope).astype(BF16)
    for t in range(9):
        out_ref[t * MID : (t + 1) * MID, :] = acc_ref[:, t * MID : (t + 1) * MID].astype(BF16)


def spans(start, count, length):
    while count:
        group, offset = divmod(start, length)
        size = min(count, length - offset)
        yield group, offset, size
        start, count = start + size, count - size


def pack_kernel(length, cores, gi_ref, g4_ref, g8_ref, gc_ref, out_ref):
    groups = out_ref.shape[0]

    def put(at, value):
        done = 0
        for group, offset, size in spans(at, value.shape[0], length):
            out_ref[group, offset : offset + size, :] = value[done : done + size]
            done += size
        return at + done

    at = 0
    for t in range(gi_ref.shape[1] // MID):
        at = put(at, gi_ref[:, t * MID : (t + 1) * MID].astype(BF16))
    for ref in (g4_ref, g8_ref):
        at = put(at, ref[...])
    if at < groups * length:
        put(at, jnp.zeros((groups * length - at, MID), BF16))
    half = gc_ref.shape[0] // cores
    for group in range(groups):
        core = group // (groups // cores)
        out_ref[group, length:, :] = gc_ref[core * half : (core + 1) * half, :].astype(BF16)


def unpack_kernel(part_ref, gi_ref, g4_ref, g8_ref, gc_ref):
    cores = part_ref.shape[0]
    half = gc_ref.shape[0] // cores
    length = part_ref.shape[1] - half

    def piece(at, count):
        got = [
            part_ref[core, offset : offset + size, :].astype(F32)
            for core, offset, size in spans(at, count, length)
        ]
        return got[0] if len(got) == 1 else jnp.concatenate(got, 0)

    at = 0
    for ref in (gi_ref, g4_ref, g8_ref):
        for t in range(ref.shape[1] // MID):
            ref[:, t * MID : (t + 1) * MID] = piece(at, MID)
            at += MID
    for core in range(cores):
        gc_ref[core * half : (core + 1) * half, :] = part_ref[core, length:, :].astype(F32)


def neighbour(value, axes, step):
    count = lax.axis_size(axes)
    pairs = [(i, i + step) for i in range(count) if 0 <= i + step < count]
    return lax.ppermute(value, axes, pairs)


def halos(edges, beside):
    bottom, top, right, left = edges
    up = neighbour(bottom, ROWS, 1)
    down = neighbour(top, ROWS, -1)
    right, left, beside = lax.optimization_barrier((right, left, beside))
    cb = up.shape[1]
    east = jnp.concatenate([up[:, cb - H :], right, down[:, cb - H :]], 0)
    west = jnp.concatenate([up[:, :H], left, down[:, :H]], 0)
    return (up, down, neighbour(east, COLS, 1), neighbour(west, COLS, -1)), beside


def over_devices(packed, length):
    cores, ys, plane = lax.axis_size("c"), lax.axis_size("y"), lax.axis_size(PLANE)

    def swap(v, axes):
        return lax.all_to_all(v, axes, 0, 0, tiled=True)

    def total(v):
        return jnp.sum(v.astype(F32), 0).astype(BF16)

    def copies(v, n):
        return jnp.broadcast_to(v[None], (n,) + v.shape)

    part = total(swap(packed.reshape(cores, -1, MID), "c"))
    part = total(swap(part.reshape(plane, -1, MID), PLANE))
    part = total(swap(copies(part, ys), "y"))
    main, rest = lax.optimization_barrier((part[:length], part[length:]))
    whole = swap(copies(main, plane), PLANE).reshape(-1, MID)
    whole = jnp.concatenate([whole, rest], 0)
    return lax.all_gather(whole, "c", axis=0, tiled=True).reshape(cores, -1, MID)


def local(features, labels, w_input, w_dilate4, w_dilate8, w_classes):
    chans, rows, cols = features.shape
    rb, cb = rows // B, cols // B
    px = rows * cols
    classes = w_classes.shape[0]
    conv = 2 * 9 * MID * MID * px

    a1 = jnp.dot(w_input, features.reshape(chans, px), preferred_element_type=F32)
    tile = ((rb, cb, 16, MID), BF16)
    edges = edge_shapes(rb, cb)
    h1, *sent = call(squeeze_kernel, "squeeze", [tile] + edges, 1, flops=px * MID)(a1)
    padded = ((rb + 2 * H, cb + 2 * H, 16, MID), BF16)
    weight = ((12 * MID, 2 * MID), BF16)
    ready = call(prepare_kernel, "prepare", [weight] * 4 + [((1, px), F32)], 3, flops=conv // 4)(
        w_dilate4, w_dilate8, labels
    )
    around, (w4t, w8t, w4s, w8s, order) = halos(sent, ready)
    g3, h1_pad, h2_pad, slope2, gc, *sent = call(
        forward_kernel, "forward",
        [tile, padded, ((rb + 4, cb + 4, 16, MID), BF16), ((rb + 4, cb + 4, 16, MID), F32),
         ((classes, MID), F32)] + edges,
        5 + len(SIDES), flops=4 * conv,
    )(h1, w4t, w8t, w_classes, order, *around)
    acc = pltpu.VMEM((MID, 9 * MID), F32)
    (g8,) = call(dilate8_kernel, "dilate8", [((9 * MID, MID), BF16)], 2, [acc], flops=conv)(g3, h2_pad)
    around, g8 = halos(sent, g8)
    g1, g4 = call(
        backward_kernel, "backward",
        [((MID, px), BF16), ((9 * MID, MID), BF16)],
        6 + len(SIDES),
        [pltpu.VMEM(*padded), pltpu.VMEM((rb + 2, cb + 2, 16, MID), BF16), acc],
        flops=4 * conv,
    )(g3, w4s, w8s, h1_pad, slope2, a1, *around)
    gi = lax.dot_general(
        g1.reshape(MID, rows, cols), features, (((1, 2), (1, 2)), ((), ())), preferred_element_type=F32
    )

    cores, plane = lax.axis_size("c"), lax.axis_size(PLANE)
    length = -(-MID * (chans // MID + 18) // (8 * cores * plane)) * 8
    (packed,) = call(
        lambda *refs: pack_kernel(length, cores, *refs), "pack",
        [((cores * plane, length + classes // cores, MID), BF16)], 4,
    )(gi, g4, g8, gc)
    part = over_devices(packed, length)
    return tuple(call(
        unpack_kernel, "unpack",
        [((MID, chans), F32), ((MID, 9 * MID), F32), ((MID, 9 * MID), F32), ((classes, MID), F32)], 1,
    )(part))


def solution(mesh):
    rows, cols = mesh.shape["rows"], mesh.shape["cols"]
    inner = math.gcd(rows, 8)
    torus = Mesh(mesh.devices.reshape(rows // inner, inner, cols // 2, 2), ROWS + COLS)
    return jax.shard_map(
        local,
        mesh=torus,
        in_specs=(P(None, ROWS, COLS), P(ROWS, COLS), P(), P(), P(), P()),
        out_specs=(P(), P(), P(), P()),
        check_vma=False,
    )
```

```python
import math

import jax
import jax.numpy as jnp
from jax import lax
from jax.experimental import pallas as pl
from jax.experimental.pallas import tpu as pltpu
from jax.sharding import Mesh, PartitionSpec as P

loss_weight = 0.03125
B = 4
H = 3
MID = 128
SIDES = ((1, 0), (-1, 0), (0, 1), (0, -1))
UNROLL = 4
ROWS, COLS = ("x", "z"), ("y", "c")
PLANE = ("z", "x")
F32 = jnp.float32
BF16 = jnp.bfloat16


def vmem(n):
    return [pl.BlockSpec(memory_space=pltpu.VMEM)] * n


def call(body, name, outs, n_in, scratch=(), flops=0, limit=10 << 20):
    shapes = [jax.ShapeDtypeStruct(s, d) for s, d in outs]
    size = sum(math.prod(s) * jnp.dtype(d).itemsize for s, d in outs)
    return pl.pallas_call(
        body,
        name=name,
        out_shape=shapes,
        in_specs=vmem(n_in),
        out_specs=vmem(len(outs)),
        scratch_shapes=list(scratch),
        compiler_params=pltpu.CompilerParams(vmem_limit_bytes=limit),
        cost_estimate=pl.CostEstimate(flops=flops, bytes_accessed=2 * size, transcendentals=0),
    )


def to_blocks(rows):
    cols, ch = rows[0].shape
    sub = lax.broadcasted_iota(jnp.int32, (cols // 8, 8, ch), 1)

    def pair(low, high):
        low, high = low.reshape(cols // 8, 8, ch), high.reshape(cols // 8, 8, ch)
        even = jnp.where(sub < 4, low, pltpu.roll(high, 4, 1))
        odd = jnp.where(sub < 4, pltpu.roll(low, 4, 1), high)
        return jnp.stack([even, odd], 1).reshape(cols // 4, 8, ch)

    return jnp.concatenate([pair(rows[0], rows[1]), pair(rows[2], rows[3])], 1)


def from_blocks(tile):
    blocks, _, ch = tile.shape
    sub = lax.broadcasted_iota(jnp.int32, (blocks // 2, 8, ch), 1)
    rows = []
    for half in range(2):
        v = tile[:, half * 8 : half * 8 + 8, :].reshape(blocks // 2, 2, 8, ch)
        even, odd = v[:, 0], v[:, 1]
        low = jnp.where(sub < 4, even, pltpu.roll(odd, 4, 1))
        high = jnp.where(sub < 4, pltpu.roll(even, 4, 1), odd)
        rows += [low.reshape(blocks * 4, ch), high.reshape(blocks * 4, ch)]
    return rows


def sigmoid(a):
    return 0.5 + 0.5 * jnp.tanh(0.5 * a)


def smooth(a):
    s = sigmoid(a)
    h = a * s
    return h, s + h * (1.0 - s)


def dot(a, b, ca, cb):
    return lax.dot_general(a, b, (((ca,), (cb,)), ((), ())), preferred_element_type=F32)


def edge_shapes(rb, cb):
    return [((H if dr else rb, H if dc else cb, 16, MID), BF16) for dr, dc in SIDES]


def put_edges(refs, i, row, rb):
    cb = row.shape[0]
    for ref, (dr, dc) in zip(refs, SIDES):
        piece = row[:H] if dc < 0 else row[cb - H :] if dc > 0 else row
        if dr == 0:
            ref[i] = piece
        elif dr < 0 and i < H:
            ref[i] = piece
        elif dr > 0 and i >= rb - H:
            ref[i - (rb - H)] = piece


def squeeze_kernel(a1_ref, h1_ref, *edge_refs):
    rb, cb = h1_ref.shape[0], h1_ref.shape[1]
    cols = cb * B
    for i in range(rb):
        rows = [a1_ref[:, (i * B + r) * cols : (i * B + r + 1) * cols].T for r in range(B)]
        a = to_blocks(rows)
        h = (a * sigmoid(a)).astype(BF16)
        h1_ref[i] = h
        put_edges(edge_refs, i, h, rb)


def taps(ref, row, step, col, n, slots=3):
    pieces = []
    for dy in range(slots):
        for dx in range(3):
            piece = ref[row + dy * step, col + dx * step : col + dx * step + n]
            pieces.append(piece.reshape(n * 16, piece.shape[-1]))
    return jnp.concatenate(pieces, 1)


def pair_weights(w_ref, out_ref, back):
    zero = jnp.zeros((MID, MID), BF16)
    for dy in range(4):
        for dx in range(3):
            for side in range(2):
                ky, kx = (2 - dy + side, 2 - dx) if back else (dy - side, dx)
                tap = zero
                if 0 <= ky < 3:
                    at = (3 * ky + kx) * MID
                    tap = w_ref[:, at : at + MID]
                    if not back:
                        tap = tap.astype(F32).T.astype(BF16)
                at = (3 * dy + dx) * MID
                out_ref[at : at + MID, side * MID : (side + 1) * MID] = tap


def prepare_kernel(w4_ref, w8_ref, labels_ref, w4t_ref, w8t_ref, w4s_ref, w8s_ref, order_ref):
    pair_weights(w4_ref, w4t_ref, False)
    pair_weights(w8_ref, w8t_ref, False)
    pair_weights(w4_ref, w4s_ref, True)
    pair_weights(w8_ref, w8s_ref, True)
    rows, cols = labels_ref.shape
    labels = labels_ref[...].astype(F32).T
    px = cols * B
    for i in range(rows // B):
        wide = [jnp.broadcast_to(labels[:, y : y + 1], (cols, MID)) for y in range(i * B, i * B + B)]
        order_ref[:, i * px : (i + 1) * px] = to_blocks(wide).reshape(px, MID).T[:1]


def place(axes):
    index, size = 0, 1
    for axis in axes:
        index = index * lax.axis_size(axis) + lax.axis_index(axis)
        size = size * lax.axis_size(axis)
    return index, size


def clear_outside(ref, reach):
    row, rows = place(ROWS)
    col, cols = place(COLS)

    @pl.when(row == 0)
    def _():
        ref[:reach] = jnp.zeros((reach,) + ref.shape[1:], ref.dtype)

    @pl.when(row == rows - 1)
    def _():
        ref[ref.shape[0] - reach :] = jnp.zeros((reach,) + ref.shape[1:], ref.dtype)

    side = jnp.zeros((ref.shape[0], reach) + ref.shape[2:], ref.dtype)

    @pl.when(col == 0)
    def _():
        ref[:, :reach] = side

    @pl.when(col == cols - 1)
    def _():
        ref[:, ref.shape[1] - reach :] = side


def fill(pad_ref, own_ref, halo_refs):
    rb, cb = own_ref.shape[0], own_ref.shape[1]
    up_ref, down_ref, left_ref, right_ref = halo_refs
    pad_ref[:H, H : H + cb] = up_ref[...]
    pad_ref[H : H + rb, H : H + cb] = own_ref[...]
    pad_ref[H + rb :, H : H + cb] = down_ref[...]
    pad_ref[:, :H] = left_ref[...]
    pad_ref[:, H + cb :] = right_ref[...]


def forward_kernel(own_ref, w4t_ref, w8t_ref, wc_ref, labels_ref, *refs):
    halo_refs, refs = refs[: len(SIDES)], refs[len(SIDES) :]
    g3_ref, h1_ref, h2_ref, slope2_ref, gc_ref = refs[:5]
    edge_refs = refs[5:]
    rb, cb = own_ref.shape[0], own_ref.shape[1]
    fill(h1_ref, own_ref, halo_refs)
    n = cb + 4

    def first(j, carry):
        both = jnp.dot(taps(h1_ref, 2 * j, 1, 0, n, 4), w4t_ref[...], preferred_element_type=F32)
        for side in range(2):
            i = 2 * j + side
            h, slope = smooth(both[:, side * MID : (side + 1) * MID])
            h2_ref[i] = h.astype(BF16).reshape(n, 16, MID)
            slope2_ref[i] = slope.reshape(n, 16, MID)
        return carry

    lax.fori_loop(0, (rb + 4) // 2, first, 0, unroll=UNROLL)
    clear_outside(h2_ref, 2)
    gc_ref[...] = jnp.zeros_like(gc_ref)
    px = cb * 16
    wc = wc_ref[...]
    classes = wc.shape[0]
    for start in range(0, rb, 4):
        for j in (start, start + 1):
            both = jnp.dot(taps(h2_ref, j, 2, 0, cb, 4), w8t_ref[...], preferred_element_type=F32)
            for side in range(2):
                i = j + 2 * side
                h3, slope = smooth(both[:, side * MID : (side + 1) * MID])
                h3 = h3.astype(BF16)
                expo = jnp.exp(dot(wc, h3, 1, 1))
                prob = expo / jnp.sum(expo, axis=0, keepdims=True)
                label = labels_ref[:, i * px : (i + 1) * px]
                hot = (label == lax.broadcasted_iota(jnp.int32, (classes, px), 0).astype(F32)).astype(F32)
                g4 = (loss_weight * (prob - hot)).astype(BF16)
                gc_ref[...] += jnp.dot(g4, h3, preferred_element_type=F32)
                back = dot(g4, wc, 0, 0)
                g3 = (back * slope).astype(BF16).reshape(cb, 16, MID)
                g3_ref[i] = g3
                put_edges(edge_refs, i, g3, rb)


def dilate8_kernel(g3_ref, h2_ref, out_ref, acc_ref):
    rb, cb = g3_ref.shape[0], g3_ref.shape[1]
    for i in range(rb):
        g = g3_ref[i].reshape(cb * 16, MID)
        part = dot(g, taps(h2_ref, i, 2, 0, cb), 0, 0)
        if i == 0:
            acc_ref[...] = part
        else:
            acc_ref[...] += part
    for t in range(9):
        out_ref[t * MID : (t + 1) * MID, :] = acc_ref[:, t * MID : (t + 1) * MID].astype(BF16)


def backward_kernel(own_ref, w4s_ref, w8s_ref, h1_ref, slope2_ref, a1_ref, *refs):
    halo_refs = refs[: len(SIDES)]
    g1_ref, out_ref, g3_ref, g2_ref, acc_ref = refs[len(SIDES) :]
    rb, cb = own_ref.shape[0], own_ref.shape[1]
    cols = cb * B
    fill(g3_ref, own_ref, halo_refs)
    n = cb + 2

    def second(back, i):
        g = back * slope2_ref[i + 1, 1 : 1 + n].reshape(n * 16, MID)
        g2_ref[i] = g.astype(BF16).reshape(n, 16, MID)

    for i in range(0, rb + 2, 4):
        for j in range(i, min(i + 2, rb + 2)):
            if j + 2 < rb + 2:
                both = jnp.dot(taps(g3_ref, j, 2, 0, n, 4), w8s_ref[...], preferred_element_type=F32)
                second(both[:, :MID], j)
                second(both[:, MID:], j + 2)
            else:
                one = w8s_ref[: 9 * MID, :MID]
                second(jnp.dot(taps(g3_ref, j, 2, 0, n), one, preferred_element_type=F32), j)
    clear_outside(g2_ref, 1)
    for j in range(0, rb, 2):
        both = jnp.dot(taps(g2_ref, j, 1, 0, cb, 4), w4s_ref[...], preferred_element_type=F32)
        for side in range(2):
            i = j + side
            g = g2_ref[i + 1, 1 : 1 + cb].reshape(cb * 16, MID)
            part = dot(g, taps(h1_ref, i + 2, 1, 2, cb), 0, 0)
            if i == 0:
                acc_ref[...] = part
            else:
                acc_ref[...] += part
            back = both[:, side * MID : (side + 1) * MID]
            for r, row in enumerate(from_blocks(back.reshape(cb, 16, MID))):
                at = (i * B + r) * cols
                _, slope = smooth(a1_ref[:, at : at + cols])
                g1_ref[:, at : at + cols] = (row.T * slope).astype(BF16)
    for t in range(9):
        out_ref[t * MID : (t + 1) * MID, :] = acc_ref[:, t * MID : (t + 1) * MID].astype(BF16)


def spans(start, count, length):
    while count:
        group, offset = divmod(start, length)
        size = min(count, length - offset)
        yield group, offset, size
        start, count = start + size, count - size


def pack_kernel(length, cores, gi_ref, g4_ref, g8_ref, gc_ref, kept_ref, sent_ref, out_ref):
    groups = out_ref.shape[0]

    def put(at, value):
        done = 0
        for group, offset, size in spans(at, value.shape[0], length):
            out_ref[group, offset : offset + size, :] = value[done : done + size]
            done += size
        return at + done

    at = 0
    for t in range(gi_ref.shape[1] // MID):
        at = put(at, gi_ref[:, t * MID : (t + 1) * MID].astype(BF16))
    for ref in (g4_ref, g8_ref):
        at = put(at, ref[...])
    if at < groups * length:
        put(at, jnp.zeros((groups * length - at, MID), BF16))
    half = gc_ref.shape[0] // cores
    for group in range(groups):
        core = group // (groups // cores)
        out_ref[group, length:, :] = gc_ref[core * half : (core + 1) * half, :].astype(BF16)
    me, plane = lax.axis_index("c"), groups // cores
    kept_ref[...] = out_ref[pl.ds(me * plane, plane)]
    sent_ref[...] = out_ref[pl.ds((1 - me) * plane, plane)]


def pair_kernel(kept_ref, both_ref, out_ref):
    other = both_ref[pl.ds(1 - lax.axis_index("c"), 1)].reshape(kept_ref.shape)
    out_ref[...] = (kept_ref[...].astype(F32) + other.astype(F32)).astype(BF16)


def unpack_kernel(part_ref, gi_ref, g4_ref, g8_ref, gc_ref):
    cores = part_ref.shape[0]
    half = gc_ref.shape[0] // cores
    length = part_ref.shape[1] - half

    def piece(at, count):
        got = [
            part_ref[core, offset : offset + size, :].astype(F32)
            for core, offset, size in spans(at, count, length)
        ]
        return got[0] if len(got) == 1 else jnp.concatenate(got, 0)

    at = 0
    for ref in (gi_ref, g4_ref, g8_ref):
        for t in range(ref.shape[1] // MID):
            ref[:, t * MID : (t + 1) * MID] = piece(at, MID)
            at += MID
    for core in range(cores):
        gc_ref[core * half : (core + 1) * half, :] = part_ref[core, length:, :].astype(F32)


def neighbour(value, axes, step):
    count = lax.axis_size(axes)
    pairs = [(i, i + step) for i in range(count) if 0 <= i + step < count]
    return lax.ppermute(value, axes, pairs)


def halos(edges, beside):
    bottom, top, right, left = edges
    up = neighbour(bottom, ROWS, 1)
    down = neighbour(top, ROWS, -1)
    right, left, beside = lax.optimization_barrier((right, left, beside))
    cb = up.shape[1]
    east = jnp.concatenate([up[:, cb - H :], right, down[:, cb - H :]], 0)
    west = jnp.concatenate([up[:, :H], left, down[:, :H]], 0)
    return (up, down, neighbour(east, COLS, 1), neighbour(west, COLS, -1)), beside


def over_devices(kept, sent, length):
    ys, plane = lax.axis_size("y"), lax.axis_size(PLANE)

    def swap(v, axes):
        return lax.all_to_all(v, axes, 0, 0, tiled=True)

    def total(v):
        return jnp.sum(v.astype(F32), 0).astype(BF16)

    def copies(v, n):
        return jnp.broadcast_to(v[None], (n,) + v.shape)

    both = lax.all_gather(sent.reshape(-1, MID), "c", axis=0, tiled=True).reshape((2,) + sent.shape)
    (part,) = call(pair_kernel, "pair", [(kept.shape, BF16)], 2)(kept, both)
    part = total(swap(part, PLANE))
    part = total(swap(copies(part, ys), "y"))
    main, rest = lax.optimization_barrier((part[:length], part[length:]))
    whole = swap(copies(main, plane), PLANE).reshape(-1, MID)
    whole = jnp.concatenate([whole, rest], 0)
    return lax.all_gather(whole, "c", axis=0, tiled=True).reshape(2, -1, MID)


def local(features, labels, w_input, w_dilate4, w_dilate8, w_classes):
    chans, rows, cols = features.shape
    rb, cb = rows // B, cols // B
    px = rows * cols
    classes = w_classes.shape[0]
    conv = 2 * 9 * MID * MID * px

    a1 = jnp.dot(w_input, features.reshape(chans, px), preferred_element_type=F32)
    tile = ((rb, cb, 16, MID), BF16)
    edges = edge_shapes(rb, cb)
    h1, *sent = call(squeeze_kernel, "squeeze", [tile] + edges, 1, flops=px * MID)(a1)
    padded = ((rb + 2 * H, cb + 2 * H, 16, MID), BF16)
    weight = ((12 * MID, 2 * MID), BF16)
    ready = call(prepare_kernel, "prepare", [weight] * 4 + [((1, px), F32)], 3, flops=conv // 4)(
        w_dilate4, w_dilate8, labels
    )
    around, (w4t, w8t, w4s, w8s, order) = halos(sent, ready)
    g3, h1_pad, h2_pad, slope2, gc, *sent = call(
        forward_kernel, "forward",
        [tile, padded, ((rb + 4, cb + 4, 16, MID), BF16), ((rb + 4, cb + 4, 16, MID), F32),
         ((classes, MID), F32)] + edges,
        5 + len(SIDES), flops=4 * conv,
    )(h1, w4t, w8t, w_classes, order, *around)
    acc = pltpu.VMEM((MID, 9 * MID), F32)
    (g8,) = call(dilate8_kernel, "dilate8", [((9 * MID, MID), BF16)], 2, [acc], flops=conv)(g3, h2_pad)
    around, g8 = halos(sent, g8)
    g1, g4 = call(
        backward_kernel, "backward",
        [((MID, px), BF16), ((9 * MID, MID), BF16)],
        6 + len(SIDES),
        [pltpu.VMEM(*padded), pltpu.VMEM((rb + 2, cb + 2, 16, MID), BF16), acc],
        flops=4 * conv,
    )(g3, w4s, w8s, h1_pad, slope2, a1, *around)
    gi = lax.dot_general(
        g1.reshape(MID, rows, cols), features, (((1, 2), (1, 2)), ((), ())), preferred_element_type=F32
    )

    cores, plane = lax.axis_size("c"), lax.axis_size(PLANE)
    length = -(-MID * (chans // MID + 18) // (8 * cores * plane)) * 8
    group = (length + classes // cores, MID)
    kept, sent = call(
        lambda *refs: pack_kernel(length, cores, *refs), "pack",
        [((plane,) + group, BF16)] * 2, 4, [pltpu.VMEM((cores * plane,) + group, BF16)],
    )(gi, g4, g8, gc)
    part = over_devices(kept, sent, length)
    return tuple(call(
        unpack_kernel, "unpack",
        [((MID, chans), F32), ((MID, 9 * MID), F32), ((MID, 9 * MID), F32), ((classes, MID), F32)], 1,
    )(part))


def solution(mesh):
    rows, cols = mesh.shape["rows"], mesh.shape["cols"]
    inner = math.gcd(rows, 8)
    torus = Mesh(mesh.devices.reshape(rows // inner, inner, cols // 2, 2), ROWS + COLS)
    return jax.shard_map(
        local,
        mesh=torus,
        in_specs=(P(None, ROWS, COLS), P(ROWS, COLS), P(), P(), P(), P()),
        out_specs=(P(), P(), P(), P()),
        check_vma=False,
    )
```
